256 devices in a mesh: az: 32 (over x, z_hi, core), rad: 8 (over z_lo, y).
Axes of the slice: x: 4, y: 4, z: 8 (z_hi: 4, z_lo: 2; z = z_hi * 2 + z_lo), core: 2. Of those that a mesh axis runs over, the one named last changes fastest.
Arguments:
- fields: float32 [5, 8, 512, 4096], P(None, None, 'rad', 'az'), may hold values from -6 to 6
- velocity: float32 [8, 512, 4096], P(None, 'rad', 'az'), may hold values from -0.5 to 0.5
- shifts: int32 [512], P('rad'), may hold values from 0 to 4095, as said below
- block_inverse: float32 [8, 512, 64], P(None, 'rad'), may hold values from -1 to 1, as said below
- coupling: float32 [8, 8], P(None, 'rad'), may hold values from 0.2 to 0.5
Outputs:
- updated: float32 [5, 8, 512, 4096], P(None, None, 'rad', 'az')
The draws below stay inside these ranges and needn't reach their ends.
Inputs may be any that keep to these rules, and one draw needn't show every extreme that they name: `shifts`: each radius's shift; the values 0 and 4095 both occur in every draw. `block_inverse`: entries of the given block inverses.
All inputs are finite; a program needn't handle non-finite values.
Results may differ from the reference program's by a relative error of at most 0.000075.
Values sent between devices are 32-bit elements; how exact they have to be, the bound alone decides.
A program may use at most 256 MiB of HBM per device.

```python
import jax
import jax.numpy as jnp
from jax import lax

NF = 5
NTH = 8
NPHI = 4096
R_DEV = 64
NR = 512
N_RAD = 8


def draw_shifts(key, part):
    key_one, key_two = jax.random.split(key)
    radius = jnp.arange(NR, dtype=jnp.int32)
    profile = (NPHI - 1) * 64 // (64 + radius * 256 // NR)
    jitter = jax.random.randint(key_one, (NR,), 0, NPHI // 8)
    drawn = (profile + jitter) % NPHI
    planted = jax.random.permutation(key_two, NR)
    drawn = drawn.at[planted[0]].set(NPHI - 1)
    drawn = drawn.at[planted[1]].set(0)
    return drawn.astype(jnp.int32)


def draw_block_inverse(key, part):
    key_one, key_two = jax.random.split(key)
    key_three = jax.random.fold_in(key, 7)
    diagonal = jax.random.uniform(key_one, (NTH, NR, 1), jnp.float32, 0.5, 0.9)
    spread = jnp.clip(jax.random.normal(key_two, (NTH, NR, R_DEV), jnp.float32), -2.5, 2.5) * (0.3 / R_DEV ** 0.5)
    far_corner = jax.random.uniform(key_three, (NTH, NR, 1), jnp.float32, 0.5, 0.8)
    radial = jnp.arange(NR, dtype=jnp.int32) % R_DEV
    column = jnp.arange(R_DEV, dtype=jnp.int32)
    identity = (radial[:, None] == column[None, :]).astype(jnp.float32)[None]
    corner_mask = ((radial[:, None] == 0) & (column[None, :] == R_DEV - 1) | (radial[:, None] == R_DEV - 1) & (column[None, :] == 0)).astype(jnp.float32)[None]
    rest = 1.0 - identity - corner_mask
    return identity * diagonal + corner_mask * far_corner + rest * spread


def block_scale(rng, shape, cuts, least, top_value):
    def one(dim, shards_of):
        steps = jax.random.uniform(jax.random.fold_in(jax.random.fold_in(rng, 6), dim), (shards_of,), jnp.float32, least / len(cuts), top_value / len(cuts))
        return jnp.repeat(jnp.exp(steps), shape[dim] // shards_of).reshape((-1,) + (1,) * (len(shape) - dim - 1))

    loudness = one(*cuts[0])
    for cut in cuts[1:]:
        loudness = loudness * one(*cut)
    return loudness


def normal_values(own_key, shape, width, most, cuts=(), held_as=jnp.bfloat16):
    values = width * jax.random.normal(own_key, shape, jnp.float32)
    if cuts:
        values = values * block_scale(own_key, shape, cuts, -0.22, 0.18)
    return jnp.clip(values, -most, most).astype(held_as)


def setup_inputs(seed: int = 0) -> dict:
    streams_of = jax.random.split(jax.random.key(seed), 6)
    return {
        "fields": normal_values(streams_of[0], (NF, NTH, NR, NPHI), 1.0, 6.0, ((2, 8), (3, 32)), jnp.float32),
        "velocity": jnp.clip(jax.random.uniform(streams_of[1], (NTH, NR, NPHI), jnp.float32, -0.5, 0.5) * block_scale(streams_of[1], (NTH, NR, NPHI), ((1, 8), (2, 32)), -0.4, 0.0), -0.5, 0.5),
        "shifts": draw_shifts(jax.random.fold_in(streams_of[5], 71), 0),
        "block_inverse": draw_block_inverse(jax.random.fold_in(streams_of[5], 71), 0),
        "coupling": jnp.clip(0.2 + 0.3 * jax.random.uniform(streams_of[4], (NTH, N_RAD), jnp.float32) ** block_scale(streams_of[4], (NTH, N_RAD), ((1, 8),), -0.2, 0.2), 0.2, 0.5),
    }


def roll_rows(values, amounts):
    return jax.vmap(lambda one_row, amount: jnp.roll(one_row, amount, axis=-1), in_axes=(2, 0), out_axes=2)(values, amounts)


def interface_solve(first_row, last_row, top_left, top_right, low_left, low_right, link_rates):
    band_count = link_rates.shape[1]
    crossings = band_count - 1
    nothing = jnp.zeros_like(first_row[:, 0])
    flat_zero = jnp.zeros_like(link_rates[:, :1])
    carry_base = nothing
    carry_slope = flat_zero
    records = []
    for crossing in range(crossings):
        if crossing > 0:
            back_link = (link_rates[:, crossing - 1] * low_left[:, crossing])[:, None]
        else:
            back_link = flat_zero
        self_link = (link_rates[:, crossing] * low_right[:, crossing])[:, None]
        fore_link = (link_rates[:, crossing] * top_left[:, crossing + 1])[:, None]
        if crossing + 1 < crossings:
            next_link = (link_rates[:, crossing + 1] * top_right[:, crossing + 1])[:, None]
        else:
            next_link = flat_zero
        steepness = back_link * carry_slope + self_link
        offset = last_row[:, crossing] + back_link * carry_base
        denominator = 1.0 - fore_link * steepness
        upper_base = (first_row[:, crossing + 1] + fore_link * offset) / denominator
        upper_slope = next_link / denominator
        carry_base = offset + steepness * upper_base
        carry_slope = steepness * upper_slope
        records.append((carry_base, carry_slope, upper_base, upper_slope))
    lower_values = [nothing] * crossings
    upper_values = [nothing] * crossings
    follow = nothing
    for crossing in reversed(range(crossings)):
        carry_base, carry_slope, upper_base, upper_slope = records[crossing]
        lower_values[crossing] = carry_base + carry_slope * follow
        upper_values[crossing] = upper_base + upper_slope * follow
        follow = upper_values[crossing]
    before = jnp.stack([nothing] + lower_values, axis=1)
    beyond = jnp.stack(upper_values + [nothing], axis=1)
    return before, beyond


def reference(fields, velocity, shifts, block_inverse, coupling):
    rotated = roll_rows(fields, shifts)
    speed = velocity[None]
    ahead_cells = jnp.roll(rotated, -1, axis=3)
    outflow = jnp.maximum(speed, 0.0) * rotated + jnp.minimum(speed, 0.0) * ahead_cells
    transported = rotated - (outflow - jnp.roll(outflow, 1, axis=3))
    energy = transported[4].reshape(NTH, N_RAD, R_DEV, NPHI)
    blocks = block_inverse.reshape(NTH, N_RAD, R_DEV, R_DEV)
    local_part = jnp.einsum('zjrl,zjlp->zjrp', blocks, energy, precision=lax.Precision.HIGHEST)
    before, beyond = interface_solve(local_part[:, :, 0, :], local_part[:, :, -1, :], blocks[:, :, 0, 0], blocks[:, :, 0, -1], blocks[:, :, -1, 0], blocks[:, :, -1, -1], coupling)
    link_prev = jnp.concatenate([jnp.zeros_like(coupling[:, :1]), coupling[:, :-1]], axis=1)
    diffused = local_part + (link_prev[:, :, None] * blocks[:, :, :, 0])[..., None] * before[:, :, None, :] + (coupling[:, :, None] * blocks[:, :, :, -1])[..., None] * beyond[:, :, None, :]
    diffused = diffused.reshape(NTH, NR, NPHI)
    return jnp.concatenate([transported[:4], diffused[None]], axis=0)
```

```python
import functools

import jax
import jax.numpy as jnp
from jax import lax
from jax.experimental import pallas as pl
from jax.experimental.pallas import tpu as pltpu
from jax.sharding import PartitionSpec as P

MESH = pl.DeviceIdType.MESH
LANES = 128
F32 = jnp.float32


def lane_index():
    return lax.broadcasted_iota(jnp.int32, (8, LANES), 1)


def kernel(az, rad, nf, rows, *refs):
    nth = 8
    own = rows // az
    order = [nf - 1] + list(range(nf - 1))
    (f_hbm, v_hbm, shifts_hbm, g_hbm, link_hbm, out) = refs[:6]
    (raw, raw_v, g, staged, turned, arrived, speed, energy, local) = refs[6:15]
    (edge, edge_in, speed_edge, speed_edge_in) = refs[15:19]
    (corner, corner_in, ends, ends_in, joined) = refs[19:24]
    (shifts, link) = refs[24:26]
    (in_sem, par_sem, send_a, recv_a, send_b, recv_b, send_e, recv_e, send_r, recv_r) = refs[26:36]
    homes = refs[36 : 36 + nf]

    me = lax.axis_index("az")
    band = lax.axis_index("rad")
    right = lax.rem(me + 1, az)
    left = lax.rem(me + az - 1, az)
    lane = lane_index()

    loads = [pltpu.make_async_copy(f_hbm.at[f], raw.at[i], in_sem.at[i]) for i, f in enumerate(order)]
    params = [
        pltpu.make_async_copy(v_hbm, raw_v, par_sem.at[0]),
        pltpu.make_async_copy(g_hbm, g, par_sem.at[1]),
        pltpu.make_async_copy(shifts_hbm, shifts, par_sem.at[2]),
        pltpu.make_async_copy(link_hbm, link, par_sem.at[3]),
    ]
    for copy in loads[:1] + params + loads[1:]:
        copy.start()

    barrier = pltpu.get_barrier_semaphore()

    def greet_az(k, carry):
        pl.semaphore_signal(barrier, 1, device_id={"az": lax.rem(me + k, az), "rad": band}, device_id_type=MESH)
        return carry

    def greet_rad(k, carry):
        pl.semaphore_signal(barrier, 1, device_id={"az": me, "rad": lax.rem(band + k, rad)}, device_id_type=MESH)
        return carry

    lax.fori_loop(1, az, greet_az, 0)
    lax.fori_loop(1, rad, greet_rad, 0)

    def stage(i):
        loads[i].wait()

        def row(r, carry):
            staged[i, r] = raw[i, pl.ds(r, nth, stride=rows), :]
            return carry

        lax.fori_loop(0, rows, row, 0, unroll=8)

    def send_out(i):
        def to(k, carry):
            m = lax.rem(me + k, az)
            pltpu.make_async_remote_copy(
                staged.at[i, pl.ds(m * own, own)],
                homes[i].at[me],
                send_a.at[i],
                recv_a.at[i],
                device_id={"az": m, "rad": band},
                device_id_type=MESH,
            ).start()
            return carry

        lax.fori_loop(1, az, to, 0)
        homes[i][me] = staged[i, pl.ds(me * own, own)]

    def wait_bytes(ref, sem):
        pltpu.make_async_copy(ref, ref, sem).wait()

    def rotate(i):
        wait_bytes(homes[i].at[pl.ds(0, az - 1)], recv_a.at[i])
        for j in range(own):
            shift = shifts[me * own + j]
            hops = lax.shift_right_logical(shift, 7)
            rest = jnp.bitwise_and(shift, LANES - 1)
            carried = lane >= rest

            def block(b, previous, j=j, hops=hops, rest=rest, carried=carried):
                origin = jnp.bitwise_and(b - hops, az - 1)
                current = pltpu.roll(homes[i][origin, j], rest, 1)
                turned[i, b, j] = jnp.where(carried, current, previous)
                return current

            opening = pltpu.roll(homes[i][jnp.bitwise_and(az - 1 - hops, az - 1), j], rest, 1)
            lax.fori_loop(0, az, block, opening, unroll=8)

    def send_home(i):
        def to(k, carry):
            m = lax.rem(me + k, az)
            pltpu.make_async_remote_copy(
                turned.at[i, m],
                arrived.at[i, pl.ds(me * own, own)],
                send_b.at[i],
                recv_b.at[i],
                device_id={"az": m, "rad": band},
                device_id_type=MESH,
            ).start()
            return carry

        lax.fori_loop(1, az, to, 0)
        arrived[i, pl.ds(me * own, own)] = turned[i, me]

    key = jnp.bitwise_and(lax.shift_right_logical(lane + 1, 1), LANES // 2 - 1)

    def packed(load):
        def row(r, carry):
            return jnp.where(key == r, pltpu.roll(load(r), 2 * r, 1), carry)

        return lax.fori_loop(0, rows, row, jnp.zeros((8, LANES), F32), unroll=8)

    def edge_copies(i):
        return [
            pltpu.make_async_remote_copy(
                edge.at[i],
                edge_in.at[i, side],
                send_e.at[i],
                recv_e.at[i],
                device_id={"az": to, "rad": band},
                device_id_type=MESH,
            )
            for side, to in enumerate((right, left))
        ]

    def send_edges(i):
        wait_bytes(arrived.at[i, pl.ds(0, rows - own)], recv_b.at[i])
        edge[i] = packed(lambda r: arrived[i, r])
        for copy in edge_copies(i):
            copy.start()

    def speed_copy():
        return pltpu.make_async_remote_copy(
            speed_edge,
            speed_edge_in,
            send_e.at[nf],
            recv_e.at[nf],
            device_id={"az": right, "rad": band},
            device_id_type=MESH,
        )

    def to_bands(source, target, which, start):
        def to(k, carry):
            copy = pltpu.make_async_remote_copy(
                source,
                target.at[band],
                send_r.at[which],
                recv_r.at[which],
                device_id={"az": me, "rad": lax.rem(band + k, rad)},
                device_id_type=MESH,
            )
            copy.start()
            return carry

        lax.fori_loop(1, rad, to, 0)

    def advect(i):
        wait_bytes(edge_in.at[i], recv_e.at[i])
        own_edge = edge[i]
        from_left = pltpu.roll(edge_in[i, 0], 2, 1)
        from_right = edge_in[i, 1]
        speed_left = pltpu.roll(speed_edge_in[...], 2, 1)
        first = pltpu.roll(own_edge, 1, 1)
        entering = jnp.maximum(speed_left, 0.0) * from_left + jnp.minimum(speed_left, 0.0) * first
        sides = jnp.where(jnp.bitwise_and(lane, 1) == 1, entering, from_right)

        def row(r, carry):
            side = pltpu.roll(sides, LANES - 1 - 2 * r, 1)
            value = arrived[i, r]
            rate = speed[r]
            ahead = jnp.where(lane == LANES - 1, side, pltpu.roll(value, LANES - 1, 1))
            outflow = jnp.maximum(rate, 0.0) * value + jnp.minimum(rate, 0.0) * ahead
            inflow = jnp.where(lane == 0, side, pltpu.roll(outflow, 1, 1))
            moved = value - (outflow - inflow)
            if i == 0:
                energy[pl.ds(r, nth, stride=rows), :] = moved
            else:
                out[order[i], pl.ds(r, nth, stride=rows), :] = moved
            return carry

        lax.fori_loop(0, rows, row, 0, unroll=8)

    def solve_local():
        for z in range(nth):
            part = jnp.dot(
                g[z],
                energy[z * rows : (z + 1) * rows, :],
                precision=lax.Precision.HIGHEST,
                preferred_element_type=F32,
            )
            local[z] = part
            ends[0, z : z + 1, :] = part[:1]
            ends[1, z : z + 1, :] = part[rows - 1 :]
        ends_in[band] = ends[...]
        to_bands(ends, ends_in, 1, True)

    def interface():
        wait_bytes(corner_in.at[pl.ds(0, rad - 1)], recv_r.at[0])
        wait_bytes(ends_in.at[pl.ds(0, rad - 1)], recv_r.at[1])
        top_left, top_right, low_left, low_right, rates = (
            [corner_in[k][:, c : c + 1] for k in range(rad)] for c in range(5)
        )
        crossings = rad - 1
        zero = jnp.zeros((8, 1), F32)
        nothing = jnp.zeros((8, LANES), F32)
        base, slope = nothing, zero
        records = []
        for k in range(crossings):
            back = rates[k - 1] * low_left[k] if k > 0 else zero
            here = rates[k] * low_right[k]
            fore = rates[k] * top_left[k + 1]
            onward = rates[k + 1] * top_right[k + 1] if k + 1 < crossings else zero
            steep = back * slope + here
            offset = ends_in[k, 1] + back * base
            scale = 1.0 - fore * steep
            upper_base = (ends_in[k + 1, 0] + fore * offset) / scale
            upper_slope = onward / scale
            base = offset + steep * upper_base
            slope = steep * upper_slope
            records.append((base, slope, upper_base, upper_slope))
        follow = nothing
        joined[0, 0] = nothing
        joined[rad - 1, 1] = nothing
        for k in reversed(range(crossings)):
            base, slope, upper_base, upper_slope = records[k]
            joined[k + 1, 0] = rates[k] * (base + slope * follow)
            follow = upper_base + upper_slope * follow
            joined[k, 1] = rates[k] * follow
        before = joined[band, 0]
        beyond = joined[band, 1]
        for z in range(nth):
            block = g[z]
            out[nf - 1, z * rows : (z + 1) * rows, :] = (
                local[z] + block[:, :1] * before[z : z + 1] + block[:, rows - 1 :] * beyond[z : z + 1]
            )

    def prepare():
        for copy in params:
            copy.wait()

        def row(r, carry):
            speed[r] = raw_v[pl.ds(r, nth, stride=rows), :]
            return carry

        lax.fori_loop(0, rows, row, 0, unroll=8)
        speed_edge[...] = packed(lambda r: speed[r])
        speed_copy().start()
        sub = lax.broadcasted_iota(jnp.int32, (8, LANES), 0)
        table = jnp.zeros((8, LANES), F32)
        for z in range(nth):
            block = g[z]
            entries = [block[0:1, 0:1], block[0:1, rows - 1 :], block[rows - 1 :, 0:1], block[rows - 1 :, rows - 1 :]]
            for c, entry in enumerate(entries):
                table = jnp.where((sub == z) & (lane == c), entry, table)
            table = jnp.where((sub == z) & (lane == 4), link[z], table)
        corner[...] = table
        corner_in[band] = table
        to_bands(corner, corner_in, 0, True)

    stage(0)
    pl.semaphore_wait(barrier, az - 1 + rad - 1)
    send_out(0)
    stage(1)
    send_out(1)
    prepare()
    for i in range(2, nf):
        stage(i)
    for i in range(nf):
        rotate(i)
        send_home(i)
        if i + 2 < nf:
            send_out(i + 2)
        if i == 2:
            wait_bytes(speed_edge_in, recv_e.at[nf])
            advect(0)
            solve_local()
        if i == 4:
            interface()
        if i > 2:
            advect(i - 2)
        if i >= 1:
            send_edges(i - 1)
    send_edges(nf - 1)
    advect(nf - 2)
    advect(nf - 1)

    for i in range(nf):
        wait_bytes(staged.at[i, pl.ds(0, rows - own)], send_a.at[i])
        wait_bytes(turned.at[i, pl.ds(0, az - 1)], send_b.at[i])
        wait_bytes(edge_in.at[i], send_e.at[i])
    wait_bytes(speed_edge, send_e.at[nf])
    wait_bytes(corner_in.at[pl.ds(0, rad - 1)], send_r.at[0])
    wait_bytes(ends_in.at[pl.ds(0, rad - 1)], send_r.at[1])


def per_device(az, rad, fields, velocity, shifts, block_inverse, coupling):
    nf, nth, rows, lanes = fields.shape
    own = rows // az
    whole = nth * rows
    hbm = pl.BlockSpec(memory_space=pltpu.MemorySpace.HBM)
    vmem = pl.BlockSpec(memory_space=pltpu.MemorySpace.VMEM)
    dma = pltpu.SemaphoreType.DMA
    out = pl.pallas_call(
        functools.partial(kernel, az, rad, nf, rows),
        out_shape=jax.ShapeDtypeStruct((nf, whole, lanes), F32),
        in_specs=[hbm] * 5,
        out_specs=vmem,
        scratch_shapes=[
            pltpu.VMEM((nf, whole, lanes), F32),
            pltpu.VMEM((whole, lanes), F32),
            pltpu.VMEM((nth, rows, rows), F32),
            pltpu.VMEM((nf, rows, nth, lanes), F32),
            pltpu.VMEM((nf, az, own, nth, lanes), F32),
            pltpu.VMEM((nf, rows, nth, lanes), F32),
            pltpu.VMEM((rows, nth, lanes), F32),
            pltpu.VMEM((whole, lanes), F32),
            pltpu.VMEM((nth, rows, lanes), F32),
            pltpu.VMEM((nf, nth, lanes), F32),
            pltpu.VMEM((nf, 2, nth, lanes), F32),
            pltpu.VMEM((nth, lanes), F32),
            pltpu.VMEM((nth, lanes), F32),
            pltpu.VMEM((nth, lanes), F32),
            pltpu.VMEM((rad, nth, lanes), F32),
            pltpu.VMEM((2, nth, lanes), F32),
            pltpu.VMEM((rad, 2, nth, lanes), F32),
            pltpu.VMEM((rad, 2, nth, lanes), F32),
            pltpu.SMEM((rows,), jnp.int32),
            pltpu.SMEM((nth,), F32),
            dma((nf,)),
            dma((4,)),
            dma((nf,)),
            dma((nf,)),
            dma((nf,)),
            dma((nf,)),
            dma((nf + 1,)),
            dma((nf + 1,)),
            dma((2,)),
            dma((2,)),
        ]
        + [pltpu.VMEM((az, own, nth, lanes), F32)] * nf,
        compiler_params=pltpu.CompilerParams(
            collective_id=0, has_side_effects=True, vmem_limit_bytes=40 << 20
        ),
    )(
        fields.reshape(nf, whole, lanes),
        velocity.reshape(whole, lanes),
        shifts,
        block_inverse,
        coupling.reshape(nth),
    )
    return out.reshape(fields.shape)


def solution(mesh):
    placed = (
        P(None, None, "rad", "az"),
        P(None, "rad", "az"),
        P("rad"),
        P(None, "rad", None),
        P(None, "rad"),
    )
    return jax.shard_map(
        functools.partial(per_device, mesh.shape["az"], mesh.shape["rad"]),
        mesh=mesh,
        in_specs=placed,
        out_specs=P(None, None, "rad", "az"),
        check_vma=False,
    )
```

```python
import functools

import jax
import jax.numpy as jnp
from jax import lax
from jax.experimental import pallas as pl
from jax.experimental.pallas import tpu as pltpu
from jax.sharding import PartitionSpec as P

MESH = pl.DeviceIdType.MESH
LANES = 128
F32 = jnp.float32


def lane_index():
    return lax.broadcasted_iota(jnp.int32, (8, LANES), 1)


def kernel(az, rad, nf, rows, *refs):
    nth = 8
    own = rows // az
    order = [nf - 1] + list(range(nf - 1))
    groups = [[0], list(range(1, nf - 1)), [nf - 1]]
    nrims = len(groups)
    (f_hbm, v_hbm, shifts_hbm, g_hbm, link_hbm, out) = refs[:6]
    (raw, raw_v, g, staged, turned, arrived, speed, energy, local) = refs[6:15]
    (rim, rim_in, speed_edge, speed_edge_in, speed_back) = refs[15:20]
    (corner, corner_in, ends, ends_in, joined) = refs[20:25]
    (shifts, link) = refs[25:27]
    (in_sem, par_sem, send_a, recv_a, send_b, recv_b, send_e, recv_e, send_r, recv_r) = refs[27:37]
    homes = refs[37 : 37 + nf]

    me = lax.axis_index("az")
    band = lax.axis_index("rad")
    right = lax.rem(me + 1, az)
    left = lax.rem(me + az - 1, az)
    lane = lane_index()

    loads = [pltpu.make_async_copy(f_hbm.at[f], raw.at[i], in_sem.at[i]) for i, f in enumerate(order)]
    params = [
        pltpu.make_async_copy(v_hbm, raw_v, par_sem.at[0]),
        pltpu.make_async_copy(g_hbm, g, par_sem.at[1]),
        pltpu.make_async_copy(shifts_hbm, shifts, par_sem.at[2]),
        pltpu.make_async_copy(link_hbm, link, par_sem.at[3]),
    ]
    for copy in loads[:1] + params + loads[1:]:
        copy.start()

    barrier = pltpu.get_barrier_semaphore()

    def greet_az(k, carry):
        pl.semaphore_signal(barrier, 1, device_id={"az": lax.rem(me + k, az), "rad": band}, device_id_type=MESH)
        return carry

    def greet_rad(k, carry):
        pl.semaphore_signal(barrier, 1, device_id={"az": me, "rad": lax.rem(band + k, rad)}, device_id_type=MESH)
        return carry

    lax.fori_loop(1, az, greet_az, 0)
    lax.fori_loop(1, rad, greet_rad, 0)

    def stage(i):
        loads[i].wait()

        def row(r, carry):
            staged[i, r] = raw[i, pl.ds(r, nth, stride=rows), :]
            return carry

        lax.fori_loop(0, rows, row, 0, unroll=8)

    def send_out(i):
        def to(k, carry):
            m = lax.rem(me + k, az)
            pltpu.make_async_remote_copy(
                staged.at[i, pl.ds(m * own, own)],
                homes[i].at[me],
                send_a.at[i],
                recv_a.at[i],
                device_id={"az": m, "rad": band},
                device_id_type=MESH,
            ).start()
            return carry

        lax.fori_loop(1, az, to, 0)
        homes[i][me] = staged[i, pl.ds(me * own, own)]

    def wait_bytes(ref, sem):
        pltpu.make_async_copy(ref, ref, sem).wait()

    def rotate(i):
        wait_bytes(homes[i].at[pl.ds(0, az - 1)], recv_a.at[i])
        shift = [shifts[me * own + j] for j in range(own)]
        hops = [lax.shift_right_logical(v, 7) for v in shift]
        rest = [jnp.bitwise_and(v, LANES - 1) for v in shift]
        carried = [lane >= v for v in rest]

        def turn(b, j):
            return pltpu.roll(homes[i][jnp.bitwise_and(b + az - hops[j], az - 1), j], rest[j], 1)

        def block(b, carry):
            ahead = jnp.bitwise_and(b + 1, az - 1)
            behind = jnp.bitwise_and(b + az - 1, az - 1)
            made = []
            for j in range(own):
                previous, lefts, rights = carry[j]
                current = turn(b, j)
                value = jnp.where(carried[j], current, previous)
                turned[i, b, j] = value
                lefts = jnp.where(lane == ahead, pltpu.roll(value, ahead + 1, 1), lefts)
                rights = jnp.where(lane == behind, pltpu.roll(value, behind, 1), rights)
                made.append((current, lefts, rights))
            return tuple(made)

        zero = jnp.zeros((8, LANES), F32)
        opening = tuple((turn(az - 1, j), zero, zero) for j in range(own))
        done = lax.fori_loop(0, az, block, opening, unroll=4)
        return [tile for j in range(own) for tile in done[j][1:]]

    def send_home(i):
        def to(k, carry):
            m = lax.rem(me + k, az)
            pltpu.make_async_remote_copy(
                turned.at[i, m],
                arrived.at[i, pl.ds(me * own, own)],
                send_b.at[i],
                recv_b.at[i],
                device_id={"az": m, "rad": band},
                device_id_type=MESH,
            ).start()
            return carry

        lax.fori_loop(1, az, to, 0)
        arrived[i, pl.ds(me * own, own)] = turned[i, me]

    key = jnp.bitwise_and(lax.shift_right_logical(lane + 1, 1), LANES // 2 - 1)

    def packed(load):
        def row(r, carry):
            return jnp.where(key == r, pltpu.roll(load(r), 2 * r, 1), carry)

        return lax.fori_loop(0, rows, row, jnp.zeros((8, LANES), F32), unroll=8)

    def send_rims(n, tiles):
        tiles = tiles + [jnp.zeros((8, LANES), F32)] * (LANES // 8 - len(tiles))
        rows_out = jnp.transpose(jnp.concatenate(tiles, axis=0))
        for b in range(az):
            rim[n, b] = rows_out[b : b + 1]

        def to(k, carry):
            m = lax.rem(me + k, az)
            pltpu.make_async_remote_copy(
                rim.at[n, m],
                rim_in.at[n, me],
                send_e.at[n],
                recv_e.at[n],
                device_id={"az": m, "rad": band},
                device_id_type=MESH,
            ).start()
            return carry

        lax.fori_loop(1, az, to, 0)
        rim_in[n, me] = rim[n, me]

    def take_rims(n):
        wait_bytes(rim_in.at[n, pl.ds(0, az - 1)], recv_e.at[n])
        tiles = [rim_in[n, m] for m in range(az)] + [jnp.zeros((LANES - az, LANES), F32)]
        return jnp.transpose(jnp.concatenate(tiles, axis=0))

    def speed_copy():
        return pltpu.make_async_remote_copy(
            speed_edge,
            speed_edge_in,
            send_e.at[nrims],
            recv_e.at[nrims],
            device_id={"az": right, "rad": band},
            device_id_type=MESH,
        )

    def to_bands(source, target, which, start):
        def to(k, carry):
            copy = pltpu.make_async_remote_copy(
                source,
                target.at[band],
                send_r.at[which],
                recv_r.at[which],
                device_id={"az": me, "rad": lax.rem(band + k, rad)},
                device_id_type=MESH,
            )
            copy.start()
            return carry

        lax.fori_loop(1, rad, to, 0)

    def advect(i, rims):
        wait_bytes(arrived.at[i, pl.ds(0, rows - own)], recv_b.at[i])

        def home(m, carry):
            for j in range(own):
                r = m * own + j
                value = arrived[i, r]
                rate, rate_back = speed[r], speed_back[r]
                left, right = rims[2 * j], rims[2 * j + 1]
                ahead = jnp.where(
                    lane == LANES - 1, pltpu.roll(right, LANES - 1 - m, 1), pltpu.roll(value, LANES - 1, 1)
                )
                back = jnp.where(
                    lane == 0, pltpu.roll(left, jnp.bitwise_and(LANES - m, LANES - 1), 1), pltpu.roll(value, 1, 1)
                )
                outflow = jnp.maximum(rate, 0.0) * value + jnp.minimum(rate, 0.0) * ahead
                inflow = jnp.maximum(rate_back, 0.0) * back + jnp.minimum(rate_back, 0.0) * value
                moved = value - (outflow - inflow)
                if i == 0:
                    energy[pl.ds(r, nth, stride=rows), :] = moved
                else:
                    out[order[i], pl.ds(r, nth, stride=rows), :] = moved
            return carry

        lax.fori_loop(0, az, home, 0, unroll=4)

    def rims_of(table, place):
        at = place * 2 * own * 8
        return [table[at + 8 * c : at + 8 * (c + 1)] for c in range(2 * own)]

    def back_speed():
        wait_bytes(speed_edge_in, recv_e.at[nrims])

        def row(r, carry):
            entry = pltpu.roll(speed_edge_in[...], jnp.bitwise_and(LANES + 1 - 2 * r, LANES - 1), 1)
            speed_back[r] = jnp.where(lane == 0, entry, pltpu.roll(speed[r], 1, 1))
            return carry

        lax.fori_loop(0, rows, row, 0, unroll=8)

    def solve_local():
        for z in range(nth):
            part = jnp.dot(
                g[z],
                energy[z * rows : (z + 1) * rows, :],
                precision=lax.Precision.HIGHEST,
                preferred_element_type=F32,
            )
            local[z] = part
            ends[0, z : z + 1, :] = part[:1]
            ends[1, z : z + 1, :] = part[rows - 1 :]
        ends_in[band] = ends[...]
        to_bands(ends, ends_in, 1, True)

    def interface():
        wait_bytes(corner_in.at[pl.ds(0, rad - 1)], recv_r.at[0])
        wait_bytes(ends_in.at[pl.ds(0, rad - 1)], recv_r.at[1])
        top_left, top_right, low_left, low_right, rates = (
            [corner_in[k][:, c : c + 1] for k in range(rad)] for c in range(5)
        )
        crossings = rad - 1
        zero = jnp.zeros((8, 1), F32)
        nothing = jnp.zeros((8, LANES), F32)
        base, slope = nothing, zero
        records = []
        for k in range(crossings):
            back = rates[k - 1] * low_left[k] if k > 0 else zero
            here = rates[k] * low_right[k]
            fore = rates[k] * top_left[k + 1]
            onward = rates[k + 1] * top_right[k + 1] if k + 1 < crossings else zero
            steep = back * slope + here
            offset = ends_in[k, 1] + back * base
            scale = 1.0 - fore * steep
            upper_base = (ends_in[k + 1, 0] + fore * offset) / scale
            upper_slope = onward / scale
            base = offset + steep * upper_base
            slope = steep * upper_slope
            records.append((base, slope, upper_base, upper_slope))
        follow = nothing
        joined[0, 0] = nothing
        joined[rad - 1, 1] = nothing
        for k in reversed(range(crossings)):
            base, slope, upper_base, upper_slope = records[k]
            joined[k + 1, 0] = rates[k] * (base + slope * follow)
            follow = upper_base + upper_slope * follow
            joined[k, 1] = rates[k] * follow
        before = joined[band, 0]
        beyond = joined[band, 1]
        for z in range(nth):
            block = g[z]
            out[nf - 1, z * rows : (z + 1) * rows, :] = (
                local[z] + block[:, :1] * before[z : z + 1] + block[:, rows - 1 :] * beyond[z : z + 1]
            )

    def prepare():
        for copy in params:
            copy.wait()

        def row(r, carry):
            speed[r] = raw_v[pl.ds(r, nth, stride=rows), :]
            return carry

        lax.fori_loop(0, rows, row, 0, unroll=8)
        speed_edge[...] = packed(lambda r: speed[r])
        speed_copy().start()
        sub = lax.broadcasted_iota(jnp.int32, (8, LANES), 0)
        table = jnp.zeros((8, LANES), F32)
        for z in range(nth):
            block = g[z]
            entries = [block[0:1, 0:1], block[0:1, rows - 1 :], block[rows - 1 :, 0:1], block[rows - 1 :, rows - 1 :]]
            for c, entry in enumerate(entries):
                table = jnp.where((sub == z) & (lane == c), entry, table)
            table = jnp.where((sub == z) & (lane == 4), link[z], table)
        corner[...] = table
        corner_in[band] = table
        to_bands(corner, corner_in, 0, True)

    stage(0)
    pl.semaphore_wait(barrier, az - 1 + rad - 1)
    send_out(0)
    for i in range(1, nf - 1):
        stage(i)
        send_out(i)
    prepare()
    stage(nf - 1)
    kept = []
    for i in range(nf):
        kept.append(rotate(i))
        send_home(i)
        if i == 0:
            send_out(nf - 1)
            send_rims(0, kept[0])
        if i == nf - 2:
            send_rims(1, sum(kept[1 : nf - 1], []))
        if i == nf - 1:
            send_rims(2, kept[nf - 1])
        if i == 1:
            back_speed()
        if i == 2:
            advect(0, rims_of(take_rims(0), 0))
            solve_local()
    table = take_rims(1)
    for i in range(1, nf - 1):
        advect(i, rims_of(table, i - 1))
    interface()
    advect(nf - 1, rims_of(take_rims(2), 0))

    for i in range(nf):
        wait_bytes(staged.at[i, pl.ds(0, rows - own)], send_a.at[i])
        wait_bytes(turned.at[i, pl.ds(0, az - 1)], send_b.at[i])
    for n in range(nrims):
        wait_bytes(rim.at[n, pl.ds(0, az - 1)], send_e.at[n])
    wait_bytes(speed_edge, send_e.at[nrims])
    wait_bytes(corner_in.at[pl.ds(0, rad - 1)], send_r.at[0])
    wait_bytes(ends_in.at[pl.ds(0, rad - 1)], send_r.at[1])


def per_device(az, rad, fields, velocity, shifts, block_inverse, coupling):
    nf, nth, rows, lanes = fields.shape
    own = rows // az
    whole = nth * rows
    hbm = pl.BlockSpec(memory_space=pltpu.MemorySpace.HBM)
    vmem = pl.BlockSpec(memory_space=pltpu.MemorySpace.VMEM)
    dma = pltpu.SemaphoreType.DMA
    out = pl.pallas_call(
        functools.partial(kernel, az, rad, nf, rows),
        out_shape=jax.ShapeDtypeStruct((nf, whole, lanes), F32),
        in_specs=[hbm] * 5,
        out_specs=vmem,
        scratch_shapes=[
            pltpu.VMEM((nf, whole, lanes), F32),
            pltpu.VMEM((whole, lanes), F32),
            pltpu.VMEM((nth, rows, rows), F32),
            pltpu.VMEM((nf, rows, nth, lanes), F32),
            pltpu.VMEM((nf, az, own, nth, lanes), F32),
            pltpu.VMEM((nf, rows, nth, lanes), F32),
            pltpu.VMEM((rows, nth, lanes), F32),
            pltpu.VMEM((whole, lanes), F32),
            pltpu.VMEM((nth, rows, lanes), F32),
            pltpu.VMEM((3, az, 1, lanes), F32),
            pltpu.VMEM((3, az, 1, lanes), F32),
            pltpu.VMEM((nth, lanes), F32),
            pltpu.VMEM((nth, lanes), F32),
            pltpu.VMEM((rows, nth, lanes), F32),
            pltpu.VMEM((nth, lanes), F32),
            pltpu.VMEM((rad, nth, lanes), F32),
            pltpu.VMEM((2, nth, lanes), F32),
            pltpu.VMEM((rad, 2, nth, lanes), F32),
            pltpu.VMEM((rad, 2, nth, lanes), F32),
            pltpu.SMEM((rows,), jnp.int32),
            pltpu.SMEM((nth,), F32),
            dma((nf,)),
            dma((4,)),
            dma((nf,)),
            dma((nf,)),
            dma((nf,)),
            dma((nf,)),
            dma((4,)),
            dma((4,)),
            dma((2,)),
            dma((2,)),
        ]
        + [pltpu.VMEM((az, own, nth, lanes), F32)] * nf,
        compiler_params=pltpu.CompilerParams(
            collective_id=0, has_side_effects=True, vmem_limit_bytes=61 << 20
        ),
    )(
        fields.reshape(nf, whole, lanes),
        velocity.reshape(whole, lanes),
        shifts,
        block_inverse,
        coupling.reshape(nth),
    )
    return out.reshape(fields.shape)


def solution(mesh):
    placed = (
        P(None, None, "rad", "az"),
        P(None, "rad", "az"),
        P("rad"),
        P(None, "rad", None),
        P(None, "rad"),
    )
    return jax.shard_map(
        functools.partial(per_device, mesh.shape["az"], mesh.shape["rad"]),
        mesh=mesh,
        in_specs=placed,
        out_specs=P(None, None, "rad", "az"),
        check_vma=False,
    )
```

```python
import functools

import jax
import jax.numpy as jnp
from jax import lax
from jax.experimental import pallas as pl
from jax.experimental.pallas import tpu as pltpu
from jax.sharding import PartitionSpec as P

MESH = pl.DeviceIdType.MESH
LANES = 128
F32 = jnp.float32


def lane_index():
    return lax.broadcasted_iota(jnp.int32, (8, LANES), 1)


def kernel(az, rad, nf, rows, *refs):
    nth = 8
    own = rows // az
    order = [nf - 1] + list(range(nf - 1))
    groups = [[0], list(range(1, nf - 1)), [nf - 1]]
    nrims = len(groups)
    (f_hbm, v_hbm, shifts_hbm, g_hbm, link_hbm, out) = refs[:6]
    (raw, raw_v, g, staged, turned, arrived, speed, energy, local) = refs[6:15]
    (rim, rim_in, speed_edge, speed_edge_in, speed_back) = refs[15:20]
    (corner, corner_in, ends, ends_in, joined) = refs[20:25]
    (shifts, link) = refs[25:27]
    (in_sem, par_sem, send_a, recv_a, send_b, recv_b, send_e, recv_e, send_r, recv_r) = refs[27:37]
    homes = refs[37 : 37 + nf]

    me = lax.axis_index("az")
    band = lax.axis_index("rad")
    right = lax.rem(me + 1, az)
    left = lax.rem(me + az - 1, az)
    lane = lane_index()

    loads = [pltpu.make_async_copy(f_hbm.at[f], raw.at[i], in_sem.at[i]) for i, f in enumerate(order)]
    params = [
        pltpu.make_async_copy(v_hbm, raw_v, par_sem.at[0]),
        pltpu.make_async_copy(g_hbm, g, par_sem.at[1]),
        pltpu.make_async_copy(shifts_hbm, shifts, par_sem.at[2]),
        pltpu.make_async_copy(link_hbm, link, par_sem.at[3]),
    ]
    for copy in loads[:1] + params + loads[1:]:
        copy.start()

    barrier = pltpu.get_barrier_semaphore()

    def greet_az(k, carry):
        pl.semaphore_signal(barrier, 1, device_id={"az": lax.rem(me + k, az), "rad": band}, device_id_type=MESH)
        return carry

    def greet_rad(k, carry):
        pl.semaphore_signal(barrier, 1, device_id={"az": me, "rad": lax.rem(band + k, rad)}, device_id_type=MESH)
        return carry

    lax.fori_loop(1, az, greet_az, 0)
    lax.fori_loop(1, rad, greet_rad, 0)

    def stage(i):
        loads[i].wait()

        def row(r, carry):
            staged[i, r] = raw[i, pl.ds(r, nth, stride=rows), :]
            return carry

        lax.fori_loop(0, rows, row, 0, unroll=8)

    def send_out(i):
        def to(k, carry):
            m = lax.rem(me + k, az)
            pltpu.make_async_remote_copy(
                staged.at[i, pl.ds(m * own, own)],
                homes[i].at[me],
                send_a.at[i],
                recv_a.at[i],
                device_id={"az": m, "rad": band},
                device_id_type=MESH,
            ).start()
            return carry

        lax.fori_loop(1, az, to, 0)
        homes[i][me] = staged[i, pl.ds(me * own, own)]

    def wait_bytes(ref, sem):
        pltpu.make_async_copy(ref, ref, sem).wait()

    def rotate(i):
        wait_bytes(homes[i].at[pl.ds(0, az - 1)], recv_a.at[i])
        shift = [shifts[me * own + j] for j in range(own)]
        hops = [lax.shift_right_logical(v, 7) for v in shift]
        rest = [jnp.bitwise_and(v, LANES - 1) for v in shift]
        carried = [lane >= v for v in rest]

        def turn(b, j):
            return pltpu.roll(homes[i][jnp.bitwise_and(b + az - hops[j], az - 1), j], rest[j], 1)

        def block(b, carry):
            ahead = jnp.bitwise_and(b + 1, az - 1)
            behind = jnp.bitwise_and(b + az - 1, az - 1)
            made = []
            for j in range(own):
                previous, lefts, rights = carry[j]
                current = turn(b, j)
                value = jnp.where(carried[j], current, previous)
                turned[i, b, j] = value
                lefts = jnp.where(lane == ahead, pltpu.roll(value, ahead + 1, 1), lefts)
                rights = jnp.where(lane == behind, pltpu.roll(value, behind, 1), rights)
                made.append((current, lefts, rights))
            return tuple(made)

        zero = jnp.zeros((8, LANES), F32)
        opening = tuple((turn(az - 1, j), zero, zero) for j in range(own))
        done = lax.fori_loop(0, az, block, opening, unroll=4)
        return [tile for j in range(own) for tile in done[j][1:]]

    def send_home(i):
        def to(k, carry):
            m = lax.rem(me + k, az)
            pltpu.make_async_remote_copy(
                turned.at[i, m],
                arrived.at[i, pl.ds(me * own, own)],
                send_b.at[i],
                recv_b.at[i],
                device_id={"az": m, "rad": band},
                device_id_type=MESH,
            ).start()
            return carry

        lax.fori_loop(1, az, to, 0)
        arrived[i, pl.ds(me * own, own)] = turned[i, me]

    key = jnp.bitwise_and(lax.shift_right_logical(lane + 1, 1), LANES // 2 - 1)

    def packed(load):
        def row(r, carry):
            return jnp.where(key == r, pltpu.roll(load(r), 2 * r, 1), carry)

        return lax.fori_loop(0, rows, row, jnp.zeros((8, LANES), F32), unroll=8)

    def send_rims(n, tiles):
        tiles = tiles + [jnp.zeros((8, LANES), F32)] * (LANES // 8 - len(tiles))
        rows_out = jnp.transpose(jnp.concatenate(tiles, axis=0))
        for b in range(az):
            rim[n, b] = rows_out[b : b + 1]

        def to(k, carry):
            m = lax.rem(me + k, az)
            pltpu.make_async_remote_copy(
                rim.at[n, m],
                rim_in.at[n, me],
                send_e.at[n],
                recv_e.at[n],
                device_id={"az": m, "rad": band},
                device_id_type=MESH,
            ).start()
            return carry

        lax.fori_loop(1, az, to, 0)
        rim_in[n, me] = rim[n, me]

    def take_rims(n):
        wait_bytes(rim_in.at[n, pl.ds(0, az - 1)], recv_e.at[n])
        tiles = [rim_in[n, m] for m in range(az)] + [jnp.zeros((LANES - az, LANES), F32)]
        return jnp.transpose(jnp.concatenate(tiles, axis=0))

    def speed_copy():
        return pltpu.make_async_remote_copy(
            speed_edge,
            speed_edge_in,
            send_e.at[nrims],
            recv_e.at[nrims],
            device_id={"az": right, "rad": band},
            device_id_type=MESH,
        )

    def to_bands(source, target, which, start):
        def to(k, carry):
            copy = pltpu.make_async_remote_copy(
                source,
                target.at[band],
                send_r.at[which],
                recv_r.at[which],
                device_id={"az": me, "rad": lax.rem(band + k, rad)},
                device_id_type=MESH,
            )
            copy.start()
            return carry

        lax.fori_loop(1, rad, to, 0)

    def advect(i, rims):
        wait_bytes(arrived.at[i, pl.ds(0, rows - own)], recv_b.at[i])

        def home(m, carry):
            for j in range(own):
                r = m * own + j
                value = arrived[i, r]
                rate, rate_back = speed[r], speed_back[r]
                left, right = rims[2 * j], rims[2 * j + 1]
                ahead = jnp.where(
                    lane == LANES - 1, pltpu.roll(right, LANES - 1 - m, 1), pltpu.roll(value, LANES - 1, 1)
                )
                back = jnp.where(
                    lane == 0, pltpu.roll(left, jnp.bitwise_and(LANES - m, LANES - 1), 1), pltpu.roll(value, 1, 1)
                )
                outflow = jnp.maximum(rate, 0.0) * value + jnp.minimum(rate, 0.0) * ahead
                inflow = jnp.maximum(rate_back, 0.0) * back + jnp.minimum(rate_back, 0.0) * value
                moved = value - (outflow - inflow)
                if i == 0:
                    energy[pl.ds(r, nth, stride=rows), :] = moved
                else:
                    out[order[i], pl.ds(r, nth, stride=rows), :] = moved
            return carry

        lax.fori_loop(0, az, home, 0, unroll=8)

    def rims_of(table, place):
        at = place * 2 * own * 8
        return [table[at + 8 * c : at + 8 * (c + 1)] for c in range(2 * own)]

    def back_speed():
        wait_bytes(speed_edge_in, recv_e.at[nrims])

        def row(r, carry):
            entry = pltpu.roll(speed_edge_in[...], jnp.bitwise_and(LANES + 1 - 2 * r, LANES - 1), 1)
            speed_back[r] = jnp.where(lane == 0, entry, pltpu.roll(speed[r], 1, 1))
            return carry

        lax.fori_loop(0, rows, row, 0, unroll=8)

    def solve_local():
        for z in range(nth):
            part = jnp.dot(
                g[z],
                energy[z * rows : (z + 1) * rows, :],
                precision=lax.Precision.HIGHEST,
                preferred_element_type=F32,
            )
            local[z] = part
            ends[0, z : z + 1, :] = part[:1]
            ends[1, z : z + 1, :] = part[rows - 1 :]
        ends_in[band] = ends[...]
        to_bands(ends, ends_in, 1, True)

    def interface():
        wait_bytes(corner_in.at[pl.ds(0, rad - 1)], recv_r.at[0])
        wait_bytes(ends_in.at[pl.ds(0, rad - 1)], recv_r.at[1])
        top_left, top_right, low_left, low_right, rates = (
            [corner_in[k][:, c : c + 1] for k in range(rad)] for c in range(5)
        )
        crossings = rad - 1
        zero = jnp.zeros((8, 1), F32)
        nothing = jnp.zeros((8, LANES), F32)
        base, slope = nothing, zero
        records = []
        for k in range(crossings):
            back = rates[k - 1] * low_left[k] if k > 0 else zero
            here = rates[k] * low_right[k]
            fore = rates[k] * top_left[k + 1]
            onward = rates[k + 1] * top_right[k + 1] if k + 1 < crossings else zero
            steep = back * slope + here
            offset = ends_in[k, 1] + back * base
            scale = 1.0 - fore * steep
            upper_base = (ends_in[k + 1, 0] + fore * offset) / scale
            upper_slope = onward / scale
            base = offset + steep * upper_base
            slope = steep * upper_slope
            records.append((base, slope, upper_base, upper_slope))
        follow = nothing
        joined[0, 0] = nothing
        joined[rad - 1, 1] = nothing
        for k in reversed(range(crossings)):
            base, slope, upper_base, upper_slope = records[k]
            joined[k + 1, 0] = rates[k] * (base + slope * follow)
            follow = upper_base + upper_slope * follow
            joined[k, 1] = rates[k] * follow
        before = joined[band, 0]
        beyond = joined[band, 1]
        for z in range(nth):
            block = g[z]
            out[nf - 1, z * rows : (z + 1) * rows, :] = (
                local[z] + block[:, :1] * before[z : z + 1] + block[:, rows - 1 :] * beyond[z : z + 1]
            )

    def prepare():
        for copy in params:
            copy.wait()

        def row(r, carry):
            speed[r] = raw_v[pl.ds(r, nth, stride=rows), :]
            return carry

        lax.fori_loop(0, rows, row, 0, unroll=8)
        speed_edge[...] = packed(lambda r: speed[r])
        speed_copy().start()
        sub = lax.broadcasted_iota(jnp.int32, (8, LANES), 0)
        table = jnp.zeros((8, LANES), F32)
        for z in range(nth):
            block = g[z]
            entries = [block[0:1, 0:1], block[0:1, rows - 1 :], block[rows - 1 :, 0:1], block[rows - 1 :, rows - 1 :]]
            for c, entry in enumerate(entries):
                table = jnp.where((sub == z) & (lane == c), entry, table)
            table = jnp.where((sub == z) & (lane == 4), link[z], table)
        corner[...] = table
        corner_in[band] = table
        to_bands(corner, corner_in, 0, True)

    stage(0)
    pl.semaphore_wait(barrier, az - 1 + rad - 1)
    send_out(0)
    for i in range(1, nf - 1):
        stage(i)
        send_out(i)
    prepare()
    stage(nf - 1)
    kept = []
    for i in range(nf):
        kept.append(rotate(i))
        if i == 0:
            send_rims(0, kept[0])
            send_home(i)
            send_out(nf - 1)
        elif i < nf - 2:
            send_home(i)
        if i == nf - 2:
            send_rims(1, sum(kept[1 : nf - 1], []))
            send_home(i)
        if i == nf - 1:
            send_rims(2, kept[nf - 1])
            send_home(i)
        if i == 1:
            back_speed()
        if i == 2:
            advect(0, rims_of(take_rims(0), 0))
            solve_local()
    table = take_rims(1)
    for i in range(1, nf - 1):
        advect(i, rims_of(table, i - 1))
    interface()
    advect(nf - 1, rims_of(take_rims(2), 0))

    for i in range(nf):
        wait_bytes(staged.at[i, pl.ds(0, rows - own)], send_a.at[i])
        wait_bytes(turned.at[i, pl.ds(0, az - 1)], send_b.at[i])
    for n in range(nrims):
        wait_bytes(rim.at[n, pl.ds(0, az - 1)], send_e.at[n])
    wait_bytes(speed_edge, send_e.at[nrims])
    wait_bytes(corner_in.at[pl.ds(0, rad - 1)], send_r.at[0])
    wait_bytes(ends_in.at[pl.ds(0, rad - 1)], send_r.at[1])


def per_device(az, rad, fields, velocity, shifts, block_inverse, coupling):
    nf, nth, rows, lanes = fields.shape
    own = rows // az
    whole = nth * rows
    hbm = pl.BlockSpec(memory_space=pltpu.MemorySpace.HBM)
    vmem = pl.BlockSpec(memory_space=pltpu.MemorySpace.VMEM)
    dma = pltpu.SemaphoreType.DMA
    out = pl.pallas_call(
        functools.partial(kernel, az, rad, nf, rows),
        out_shape=jax.ShapeDtypeStruct((nf, whole, lanes), F32),
        in_specs=[hbm] * 5,
        out_specs=vmem,
        scratch_shapes=[
            pltpu.VMEM((nf, whole, lanes), F32),
            pltpu.VMEM((whole, lanes), F32),
            pltpu.VMEM((nth, rows, rows), F32),
            pltpu.VMEM((nf, rows, nth, lanes), F32),
            pltpu.VMEM((nf, az, own, nth, lanes), F32),
            pltpu.VMEM((nf, rows, nth, lanes), F32),
            pltpu.VMEM((rows, nth, lanes), F32),
            pltpu.VMEM((whole, lanes), F32),
            pltpu.VMEM((nth, rows, lanes), F32),
            pltpu.VMEM((3, az, 1, lanes), F32),
            pltpu.VMEM((3, az, 1, lanes), F32),
            pltpu.VMEM((nth, lanes), F32),
            pltpu.VMEM((nth, lanes), F32),
            pltpu.VMEM((rows, nth, lanes), F32),
            pltpu.VMEM((nth, lanes), F32),
            pltpu.VMEM((rad, nth, lanes), F32),
            pltpu.VMEM((2, nth, lanes), F32),
            pltpu.VMEM((rad, 2, nth, lanes), F32),
            pltpu.VMEM((rad, 2, nth, lanes), F32),
            pltpu.SMEM((rows,), jnp.int32),
            pltpu.SMEM((nth,), F32),
            dma((nf,)),
            dma((4,)),
            dma((nf,)),
            dma((nf,)),
            dma((nf,)),
            dma((nf,)),
            dma((4,)),
            dma((4,)),
            dma((2,)),
            dma((2,)),
        ]
        + [pltpu.VMEM((az, own, nth, lanes), F32)] * nf,
        compiler_params=pltpu.CompilerParams(
            collective_id=0, has_side_effects=True, vmem_limit_bytes=40 << 20
        ),
    )(
        *(
            pltpu.with_memory_space_constraint(x, pltpu.MemorySpace.HBM)
            for x in (
                fields.reshape(nf, whole, lanes),
                velocity.reshape(whole, lanes),
                shifts,
                block_inverse,
                coupling.reshape(nth),
            )
        )
    )
    return out.reshape(fields.shape)


def solution(mesh):
    placed = (
        P(None, None, "rad", "az"),
        P(None, "rad", "az"),
        P("rad"),
        P(None, "rad", None),
        P(None, "rad"),
    )
    return jax.shard_map(
        functools.partial(per_device, mesh.shape["az"], mesh.shape["rad"]),
        mesh=mesh,
        in_specs=placed,
        out_specs=P(None, None, "rad", "az"),
        check_vma=False,
    )
```

```python
import functools

import jax
import jax.numpy as jnp
from jax import lax
from jax.experimental import pallas as pl
from jax.experimental.pallas import tpu as pltpu
from jax.sharding import PartitionSpec as P

MESH = pl.DeviceIdType.MESH
LANES = 128
F32 = jnp.float32


def lane_index():
    return lax.broadcasted_iota(jnp.int32, (8, LANES), 1)


def kernel(az, rad, nf, rows, *refs):
    nth = 8
    own = rows // az
    order = [nf - 1] + list(range(nf - 1))
    nrims = 2
    (f_hbm, v_hbm, shifts_hbm, g_hbm, link_hbm, out) = refs[:6]
    (raw, raw_v, g, staged, turned, arrived, speed, energy, local) = refs[6:15]
    (rim, rim_in, speed_edge, speed_edge_in, speed_back) = refs[15:20]
    (corner, corner_in, ends, ends_in, joined) = refs[20:25]
    (shifts, link) = refs[25:27]
    (in_sem, par_sem, send_a, recv_a, send_b, recv_b, send_e, recv_e, send_r, recv_r) = refs[27:37]
    homes = refs[37 : 37 + nf]

    me = lax.axis_index("az")
    band = lax.axis_index("rad")
    right = lax.rem(me + 1, az)
    left = lax.rem(me + az - 1, az)
    lane = lane_index()

    loads = [pltpu.make_async_copy(f_hbm.at[f], raw.at[i], in_sem.at[i]) for i, f in enumerate(order)]
    params = [
        pltpu.make_async_copy(v_hbm, raw_v, par_sem.at[0]),
        pltpu.make_async_copy(g_hbm, g, par_sem.at[1]),
        pltpu.make_async_copy(shifts_hbm, shifts, par_sem.at[2]),
        pltpu.make_async_copy(link_hbm, link, par_sem.at[3]),
    ]
    loads[0].start()

    barrier = pltpu.get_barrier_semaphore()

    def greet_az(k, carry):
        pl.semaphore_signal(barrier, 1, device_id={"az": lax.rem(me + k, az), "rad": band}, device_id_type=MESH)
        return carry

    def greet_rad(k, carry):
        pl.semaphore_signal(barrier, 1, device_id={"az": me, "rad": lax.rem(band + k, rad)}, device_id_type=MESH)
        return carry

    lax.fori_loop(1, az, greet_az, 0)
    lax.fori_loop(1, rad, greet_rad, 0)
    for copy in loads[1:] + params:
        copy.start()

    def stage(i):
        loads[i].wait()

        def row(r, carry):
            staged[i, r] = raw[i, pl.ds(r, nth, stride=rows), :]
            return carry

        lax.fori_loop(0, rows, row, 0, unroll=8)

    def send_out(i):
        def to(k, carry):
            m = lax.rem(me + k, az)
            pltpu.make_async_remote_copy(
                staged.at[i, pl.ds(m * own, own)],
                homes[i].at[me],
                send_a.at[i],
                recv_a.at[i],
                device_id={"az": m, "rad": band},
                device_id_type=MESH,
            ).start()
            return carry

        lax.fori_loop(1, az, to, 0)
        homes[i][me] = staged[i, pl.ds(me * own, own)]

    def wait_bytes(ref, sem):
        pltpu.make_async_copy(ref, ref, sem).wait()

    def rotate(i):
        wait_bytes(homes[i].at[pl.ds(0, az - 1)], recv_a.at[i])
        shift = [shifts[me * own + j] for j in range(own)]
        hops = [lax.shift_right_logical(v, 7) for v in shift]
        rest = [jnp.bitwise_and(v, LANES - 1) for v in shift]
        carried = [lane >= v for v in rest]

        def turn(b, j):
            return pltpu.roll(homes[i][jnp.bitwise_and(b + az - hops[j], az - 1), j], rest[j], 1)

        def block(b, carry):
            ahead = jnp.bitwise_and(b + 1, az - 1)
            behind = jnp.bitwise_and(b + az - 1, az - 1)
            made = []
            for j in range(own):
                previous, lefts, rights = carry[j]
                current = turn(b, j)
                value = jnp.where(carried[j], current, previous)
                turned[i, b, j] = value
                lefts = jnp.where(lane == ahead, pltpu.roll(value, ahead + 1, 1), lefts)
                rights = jnp.where(lane == behind, pltpu.roll(value, behind, 1), rights)
                made.append((current, lefts, rights))
            return tuple(made)

        zero = jnp.zeros((8, LANES), F32)
        opening = tuple((turn(az - 1, j), zero, zero) for j in range(own))
        done = lax.fori_loop(0, az, block, opening, unroll=4)
        return [tile for j in range(own) for tile in done[j][1:]]

    def send_home(i):
        def to(k, carry):
            m = lax.rem(me + k, az)
            pltpu.make_async_remote_copy(
                turned.at[i, m],
                arrived.at[i, pl.ds(me * own, own)],
                send_b.at[i],
                recv_b.at[i],
                device_id={"az": m, "rad": band},
                device_id_type=MESH,
            ).start()
            return carry

        lax.fori_loop(1, az, to, 0)
        arrived[i, pl.ds(me * own, own)] = turned[i, me]

    key = jnp.bitwise_and(lax.shift_right_logical(lane + 1, 1), LANES // 2 - 1)

    def packed(load):
        def row(r, carry):
            return jnp.where(key == r, pltpu.roll(load(r), 2 * r, 1), carry)

        return lax.fori_loop(0, rows, row, jnp.zeros((8, LANES), F32), unroll=8)

    def send_rims(n, tiles):
        tiles = tiles + [jnp.zeros((8, LANES), F32)] * (LANES // 8 - len(tiles))
        rows_out = jnp.transpose(jnp.concatenate(tiles, axis=0))
        for b in range(az):
            rim[n, b] = rows_out[b : b + 1]

        def to(k, carry):
            m = lax.rem(me + k, az)
            pltpu.make_async_remote_copy(
                rim.at[n, m],
                rim_in.at[n, me],
                send_e.at[n],
                recv_e.at[n],
                device_id={"az": m, "rad": band},
                device_id_type=MESH,
            ).start()
            return carry

        lax.fori_loop(1, az, to, 0)
        rim_in[n, me] = rim[n, me]

    def take_rims(n):
        wait_bytes(rim_in.at[n, pl.ds(0, az - 1)], recv_e.at[n])
        tiles = [rim_in[n, m] for m in range(az)] + [jnp.zeros((LANES - az, LANES), F32)]
        return jnp.transpose(jnp.concatenate(tiles, axis=0))

    def speed_copy():
        return pltpu.make_async_remote_copy(
            speed_edge,
            speed_edge_in,
            send_e.at[nrims],
            recv_e.at[nrims],
            device_id={"az": right, "rad": band},
            device_id_type=MESH,
        )

    def to_bands(source, target, which, start):
        def to(k, carry):
            copy = pltpu.make_async_remote_copy(
                source,
                target.at[band],
                send_r.at[which],
                recv_r.at[which],
                device_id={"az": me, "rad": lax.rem(band + k, rad)},
                device_id_type=MESH,
            )
            copy.start()
            return carry

        lax.fori_loop(1, rad, to, 0)

    def advect(i, rims):
        wait_bytes(arrived.at[i, pl.ds(0, rows - own)], recv_b.at[i])

        def home(m, carry):
            for j in range(own):
                r = m * own + j
                value = arrived[i, r]
                rate, rate_back = speed[r], speed_back[r]
                left, right = rims[2 * j], rims[2 * j + 1]
                ahead = jnp.where(
                    lane == LANES - 1, pltpu.roll(right, LANES - 1 - m, 1), pltpu.roll(value, LANES - 1, 1)
                )
                back = jnp.where(
                    lane == 0, pltpu.roll(left, jnp.bitwise_and(LANES - m, LANES - 1), 1), pltpu.roll(value, 1, 1)
                )
                outflow = jnp.maximum(rate, 0.0) * value + jnp.minimum(rate, 0.0) * ahead
                inflow = jnp.maximum(rate_back, 0.0) * back + jnp.minimum(rate_back, 0.0) * value
                moved = value - (outflow - inflow)
                if i == 0:
                    energy[pl.ds(r, nth, stride=rows), :] = moved
                else:
                    out[order[i], pl.ds(r, nth, stride=rows), :] = moved
            return carry

        lax.fori_loop(0, az, home, 0, unroll=8)

    def rims_of(table, place):
        at = place * 2 * own * 8
        return [table[at + 8 * c : at + 8 * (c + 1)] for c in range(2 * own)]

    def back_speed():
        wait_bytes(speed_edge_in, recv_e.at[nrims])

        def row(r, carry):
            entry = pltpu.roll(speed_edge_in[...], jnp.bitwise_and(LANES + 1 - 2 * r, LANES - 1), 1)
            speed_back[r] = jnp.where(lane == 0, entry, pltpu.roll(speed[r], 1, 1))
            return carry

        lax.fori_loop(0, rows, row, 0, unroll=8)

    def solve_local():
        for z in range(nth):
            part = jnp.dot(
                g[z],
                energy[z * rows : (z + 1) * rows, :],
                precision=lax.Precision.HIGHEST,
                preferred_element_type=F32,
            )
            local[z] = part
            ends[0, z : z + 1, :] = part[:1]
            ends[1, z : z + 1, :] = part[rows - 1 :]
        ends_in[band] = ends[...]
        to_bands(ends, ends_in, 1, True)

    def interface():
        wait_bytes(corner_in.at[pl.ds(0, rad - 1)], recv_r.at[0])
        wait_bytes(ends_in.at[pl.ds(0, rad - 1)], recv_r.at[1])
        top_left, top_right, low_left, low_right, rates = (
            [corner_in[k][:, c : c + 1] for k in range(rad)] for c in range(5)
        )
        crossings = rad - 1
        zero = jnp.zeros((8, 1), F32)
        nothing = jnp.zeros((8, LANES), F32)
        base, slope = nothing, zero
        records = []
        for k in range(crossings):
            back = rates[k - 1] * low_left[k] if k > 0 else zero
            here = rates[k] * low_right[k]
            fore = rates[k] * top_left[k + 1]
            onward = rates[k + 1] * top_right[k + 1] if k + 1 < crossings else zero
            steep = back * slope + here
            offset = ends_in[k, 1] + back * base
            scale = 1.0 - fore * steep
            upper_base = (ends_in[k + 1, 0] + fore * offset) / scale
            upper_slope = onward / scale
            base = offset + steep * upper_base
            slope = steep * upper_slope
            records.append((base, slope, upper_base, upper_slope))
        follow = nothing
        joined[0, 0] = nothing
        joined[rad - 1, 1] = nothing
        for k in reversed(range(crossings)):
            base, slope, upper_base, upper_slope = records[k]
            joined[k + 1, 0] = rates[k] * (base + slope * follow)
            follow = upper_base + upper_slope * follow
            joined[k, 1] = rates[k] * follow
        before = joined[band, 0]
        beyond = joined[band, 1]
        for z in range(nth):
            block = g[z]
            out[nf - 1, z * rows : (z + 1) * rows, :] = (
                local[z] + block[:, :1] * before[z : z + 1] + block[:, rows - 1 :] * beyond[z : z + 1]
            )

    def prepare():
        for copy in params:
            copy.wait()

        def row(r, carry):
            speed[r] = raw_v[pl.ds(r, nth, stride=rows), :]
            return carry

        lax.fori_loop(0, rows, row, 0, unroll=8)
        speed_edge[...] = packed(lambda r: speed[r])
        speed_copy().start()
        sub = lax.broadcasted_iota(jnp.int32, (8, LANES), 0)
        table = jnp.zeros((8, LANES), F32)
        for z in range(nth):
            block = g[z]
            entries = [block[0:1, 0:1], block[0:1, rows - 1 :], block[rows - 1 :, 0:1], block[rows - 1 :, rows - 1 :]]
            for c, entry in enumerate(entries):
                table = jnp.where((sub == z) & (lane == c), entry, table)
            table = jnp.where((sub == z) & (lane == 4), link[z], table)
        corner[...] = table
        corner_in[band] = table
        to_bands(corner, corner_in, 0, True)

    stage(0)
    pl.semaphore_wait(barrier, az - 1 + rad - 1)
    send_out(0)
    for i in range(1, nf - 1):
        stage(i)
        send_out(i)
    prepare()
    stage(nf - 1)
    kept = []
    for i in range(nf):
        kept.append(rotate(i))
        if i == 0:
            send_home(i)
            send_out(nf - 1)
        elif i == 1:
            send_rims(0, kept[0] + kept[1])
            send_home(i)
        elif i < nf - 2:
            send_home(i)
        if i == nf - 2:
            send_home(i)
        if i == nf - 1:
            send_rims(1, sum(kept[2:], []))
            send_home(i)
        if i == 1:
            back_speed()
        if i == 3:
            opened = take_rims(0)
            advect(0, rims_of(opened, 0))
            solve_local()
        if i == 3:
            advect(1, rims_of(opened, 1))
    table = take_rims(1)
    for i in range(2, nf - 1):
        advect(i, rims_of(table, i - 2))
    interface()
    advect(nf - 1, rims_of(table, nf - 3))

    for i in range(nf):
        wait_bytes(staged.at[i, pl.ds(0, rows - own)], send_a.at[i])
        wait_bytes(turned.at[i, pl.ds(0, az - 1)], send_b.at[i])
    for n in range(nrims):
        wait_bytes(rim.at[n, pl.ds(0, az - 1)], send_e.at[n])
    wait_bytes(speed_edge, send_e.at[nrims])
    wait_bytes(corner_in.at[pl.ds(0, rad - 1)], send_r.at[0])
    wait_bytes(ends_in.at[pl.ds(0, rad - 1)], send_r.at[1])


def per_device(az, rad, fields, velocity, shifts, block_inverse, coupling):
    nf, nth, rows, lanes = fields.shape
    own = rows // az
    whole = nth * rows
    hbm = pl.BlockSpec(memory_space=pltpu.MemorySpace.HBM)
    vmem = pl.BlockSpec(memory_space=pltpu.MemorySpace.VMEM)
    dma = pltpu.SemaphoreType.DMA
    out = pl.pallas_call(
        functools.partial(kernel, az, rad, nf, rows),
        out_shape=jax.ShapeDtypeStruct((nf, whole, lanes), F32),
        in_specs=[hbm] * 5,
        out_specs=vmem,
        scratch_shapes=[
            pltpu.VMEM((nf, whole, lanes), F32),
            pltpu.VMEM((whole, lanes), F32),
            pltpu.VMEM((nth, rows, rows), F32),
            pltpu.VMEM((nf, rows, nth, lanes), F32),
            pltpu.VMEM((nf, az, own, nth, lanes), F32),
            pltpu.VMEM((nf, rows, nth, lanes), F32),
            pltpu.VMEM((rows, nth, lanes), F32),
            pltpu.VMEM((whole, lanes), F32),
            pltpu.VMEM((nth, rows, lanes), F32),
            pltpu.VMEM((2, az, 1, lanes), F32),
            pltpu.VMEM((2, az, 1, lanes), F32),
            pltpu.VMEM((nth, lanes), F32),
            pltpu.VMEM((nth, lanes), F32),
            pltpu.VMEM((rows, nth, lanes), F32),
            pltpu.VMEM((nth, lanes), F32),
            pltpu.VMEM((rad, nth, lanes), F32),
            pltpu.VMEM((2, nth, lanes), F32),
            pltpu.VMEM((rad, 2, nth, lanes), F32),
            pltpu.VMEM((rad, 2, nth, lanes), F32),
            pltpu.SMEM((rows,), jnp.int32),
            pltpu.SMEM((nth,), F32),
            dma((nf,)),
            dma((4,)),
            dma((nf,)),
            dma((nf,)),
            dma((nf,)),
            dma((nf,)),
            dma((3,)),
            dma((3,)),
            dma((2,)),
            dma((2,)),
        ]
        + [pltpu.VMEM((az, own, nth, lanes), F32)] * nf,
        compiler_params=pltpu.CompilerParams(
            collective_id=0, has_side_effects=True, vmem_limit_bytes=40 << 20
        ),
    )(
        *(
            pltpu.with_memory_space_constraint(x, pltpu.MemorySpace.HBM)
            for x in (
                fields.reshape(nf, whole, lanes),
                velocity.reshape(whole, lanes),
                shifts,
                block_inverse,
                coupling.reshape(nth),
            )
        )
    )
    return out.reshape(fields.shape)


def solution(mesh):
    placed = (
        P(None, None, "rad", "az"),
        P(None, "rad", "az"),
        P("rad"),
        P(None, "rad", None),
        P(None, "rad"),
    )
    return jax.shard_map(
        functools.partial(per_device, mesh.shape["az"], mesh.shape["rad"]),
        mesh=mesh,
        in_specs=placed,
        out_specs=P(None, None, "rad", "az"),
        check_vma=False,
    )
```

```python
import functools

import jax
import jax.numpy as jnp
from jax import lax
from jax.experimental import pallas as pl
from jax.experimental.pallas import tpu as pltpu
from jax.sharding import PartitionSpec as P

MESH = pl.DeviceIdType.MESH
LANES = 128
F32 = jnp.float32


def lane_index():
    return lax.broadcasted_iota(jnp.int32, (8, LANES), 1)


def kernel(az, rad, nf, rows, *refs):
    nth = 8
    own = rows // az
    order = [nf - 1] + list(range(nf - 1))
    nrims = 2
    (f_hbm, v_hbm, shifts_hbm, g_hbm, link_hbm, out) = refs[:6]
    (raw, raw_v, g, staged, turned, arrived, speed, energy, local) = refs[6:15]
    (rim, rim_in, speed_edge, speed_edge_in, speed_back) = refs[15:20]
    (corner, corner_in, ends, ends_in, joined) = refs[20:25]
    (shifts, link) = refs[25:27]
    (in_sem, par_sem, send_a, recv_a, send_b, recv_b, send_e, recv_e, send_r, recv_r) = refs[27:37]
    homes = refs[37 : 37 + nf]

    me = lax.axis_index("az")
    band = lax.axis_index("rad")
    right = lax.rem(me + 1, az)
    left = lax.rem(me + az - 1, az)
    lane = lane_index()

    loads = [pltpu.make_async_copy(f_hbm.at[f], raw.at[i], in_sem.at[i]) for i, f in enumerate(order)]
    params = [
        pltpu.make_async_copy(v_hbm, raw_v, par_sem.at[0]),
        pltpu.make_async_copy(g_hbm, g, par_sem.at[1]),
        pltpu.make_async_copy(shifts_hbm, shifts, par_sem.at[2]),
        pltpu.make_async_copy(link_hbm, link, par_sem.at[3]),
    ]
    loads[0].start()

    barrier = pltpu.get_barrier_semaphore()

    def greet_az(k, carry):
        pl.semaphore_signal(barrier, 1, device_id={"az": lax.rem(me + k, az), "rad": band}, device_id_type=MESH)
        return carry

    def greet_rad(k, carry):
        pl.semaphore_signal(barrier, 1, device_id={"az": me, "rad": lax.rem(band + k, rad)}, device_id_type=MESH)
        return carry

    lax.fori_loop(1, az, greet_az, 0)
    lax.fori_loop(1, rad, greet_rad, 0)
    for copy in loads[1:] + params:
        copy.start()

    def stage(i):
        loads[i].wait()

        def row(r, carry):
            staged[i, r] = raw[i, pl.ds(r, nth, stride=rows), :]
            return carry

        lax.fori_loop(0, rows, row, 0, unroll=8)

    def send_out(i):
        def to(k, carry):
            m = lax.rem(me + k, az)
            pltpu.make_async_remote_copy(
                staged.at[i, pl.ds(m * own, own)],
                homes[i].at[me],
                send_a.at[i],
                recv_a.at[i],
                device_id={"az": m, "rad": band},
                device_id_type=MESH,
            ).start()
            return carry

        lax.fori_loop(1, az, to, 0)
        homes[i][me] = staged[i, pl.ds(me * own, own)]

    def wait_bytes(ref, sem):
        pltpu.make_async_copy(ref, ref, sem).wait()

    def rotate(i):
        wait_bytes(homes[i].at[pl.ds(0, az - 1)], recv_a.at[i])
        shift = [shifts[me * own + j] for j in range(own)]
        hops = [lax.shift_right_logical(v, 7) for v in shift]
        rest = [jnp.bitwise_and(v, LANES - 1) for v in shift]
        carried = [lane >= v for v in rest]

        def turn(b, j):
            return pltpu.roll(homes[i][jnp.bitwise_and(b + az - hops[j], az - 1), j], rest[j], 1)

        def block(b, carry):
            ahead = jnp.bitwise_and(b + 1, az - 1)
            behind = jnp.bitwise_and(b + az - 1, az - 1)
            made = []
            for j in range(own):
                previous, lefts, rights = carry[j]
                current = turn(b, j)
                value = jnp.where(carried[j], current, previous)
                turned[i, b, j] = value
                lefts = jnp.where(lane == ahead, pltpu.roll(value, ahead + 1, 1), lefts)
                rights = jnp.where(lane == behind, pltpu.roll(value, behind, 1), rights)
                made.append((current, lefts, rights))
            return tuple(made)

        zero = jnp.zeros((8, LANES), F32)
        opening = tuple((turn(az - 1, j), zero, zero) for j in range(own))
        done = lax.fori_loop(0, az, block, opening, unroll=4)
        return [tile for j in range(own) for tile in done[j][1:]]

    def send_home(i):
        def to(k, carry):
            m = lax.rem(me + k, az)
            pltpu.make_async_remote_copy(
                turned.at[i, m],
                arrived.at[i, pl.ds(me * own, own)],
                send_b.at[i],
                recv_b.at[i],
                device_id={"az": m, "rad": band},
                device_id_type=MESH,
            ).start()
            return carry

        lax.fori_loop(1, az, to, 0)
        arrived[i, pl.ds(me * own, own)] = turned[i, me]

    key = jnp.bitwise_and(lax.shift_right_logical(lane + 1, 1), LANES // 2 - 1)

    def packed(load):
        def row(r, carry):
            return jnp.where(key == r, pltpu.roll(load(r), 2 * r, 1), carry)

        return lax.fori_loop(0, rows, row, jnp.zeros((8, LANES), F32), unroll=8)

    def send_rims(n, tiles):
        tiles = tiles + [jnp.zeros((8, LANES), F32)] * (LANES // 8 - len(tiles))
        rows_out = jnp.transpose(jnp.concatenate(tiles, axis=0))
        for b in range(az):
            rim[n, b] = rows_out[b : b + 1]

        def to(k, carry):
            m = lax.rem(me + k, az)
            pltpu.make_async_remote_copy(
                rim.at[n, m],
                rim_in.at[n, me],
                send_e.at[n],
                recv_e.at[n],
                device_id={"az": m, "rad": band},
                device_id_type=MESH,
            ).start()
            return carry

        lax.fori_loop(1, az, to, 0)
        rim_in[n, me] = rim[n, me]

    def take_rims(n):
        wait_bytes(rim_in.at[n, pl.ds(0, az - 1)], recv_e.at[n])
        tiles = [rim_in[n, m] for m in range(az)] + [jnp.zeros((LANES - az, LANES), F32)]
        return jnp.transpose(jnp.concatenate(tiles, axis=0))

    def speed_copy():
        return pltpu.make_async_remote_copy(
            speed_edge,
            speed_edge_in,
            send_e.at[nrims],
            recv_e.at[nrims],
            device_id={"az": right, "rad": band},
            device_id_type=MESH,
        )

    def to_bands(source, target, which, start):
        def to(k, carry):
            copy = pltpu.make_async_remote_copy(
                source,
                target.at[band],
                send_r.at[which],
                recv_r.at[which],
                device_id={"az": me, "rad": lax.rem(band + k, rad)},
                device_id_type=MESH,
            )
            copy.start()
            return carry

        lax.fori_loop(1, rad, to, 0)

    def advect(i, rims):
        wait_bytes(arrived.at[i, pl.ds(0, rows - own)], recv_b.at[i])

        def home(m, carry):
            for j in range(own):
                r = m * own + j
                value = arrived[i, r]
                rate, rate_back = speed[r], speed_back[r]
                left, right = rims[2 * j], rims[2 * j + 1]
                ahead = jnp.where(
                    lane == LANES - 1, pltpu.roll(right, LANES - 1 - m, 1), pltpu.roll(value, LANES - 1, 1)
                )
                back = jnp.where(
                    lane == 0, pltpu.roll(left, jnp.bitwise_and(LANES - m, LANES - 1), 1), pltpu.roll(value, 1, 1)
                )
                outflow = jnp.maximum(rate, 0.0) * value + jnp.minimum(rate, 0.0) * ahead
                inflow = jnp.maximum(rate_back, 0.0) * back + jnp.minimum(rate_back, 0.0) * value
                moved = value - (outflow - inflow)
                if i == 0:
                    energy[pl.ds(r, nth, stride=rows), :] = moved
                else:
                    out[order[i], pl.ds(r, nth, stride=rows), :] = moved
            return carry

        lax.fori_loop(0, az, home, 0, unroll=8)

    def rims_of(table, place):
        at = place * 2 * own * 8
        return [table[at + 8 * c : at + 8 * (c + 1)] for c in range(2 * own)]

    def back_speed():
        wait_bytes(speed_edge_in, recv_e.at[nrims])

        def row(r, carry):
            entry = pltpu.roll(speed_edge_in[...], jnp.bitwise_and(LANES + 1 - 2 * r, LANES - 1), 1)
            speed_back[r] = jnp.where(lane == 0, entry, pltpu.roll(speed[r], 1, 1))
            return carry

        lax.fori_loop(0, rows, row, 0, unroll=8)

    def solve_local():
        for z in range(nth):
            part = jnp.dot(
                g[z],
                energy[z * rows : (z + 1) * rows, :],
                precision=lax.Precision.HIGHEST,
                preferred_element_type=F32,
            )
            local[z] = part
            ends[0, z : z + 1, :] = part[:1]
            ends[1, z : z + 1, :] = part[rows - 1 :]
        ends_in[band] = ends[...]
        to_bands(ends, ends_in, 1, True)

    def interface():
        wait_bytes(corner_in.at[pl.ds(0, rad - 1)], recv_r.at[0])
        wait_bytes(ends_in.at[pl.ds(0, rad - 1)], recv_r.at[1])
        top_left, top_right, low_left, low_right, rates = (
            [corner_in[k][:, c : c + 1] for k in range(rad)] for c in range(5)
        )
        crossings = rad - 1
        zero = jnp.zeros((8, 1), F32)
        nothing = jnp.zeros((8, LANES), F32)
        base, slope = nothing, zero
        records = []
        for k in range(crossings):
            back = rates[k - 1] * low_left[k] if k > 0 else zero
            here = rates[k] * low_right[k]
            fore = rates[k] * top_left[k + 1]
            onward = rates[k + 1] * top_right[k + 1] if k + 1 < crossings else zero
            steep = back * slope + here
            offset = ends_in[k, 1] + back * base
            scale = 1.0 - fore * steep
            upper_base = (ends_in[k + 1, 0] + fore * offset) / scale
            upper_slope = onward / scale
            base = offset + steep * upper_base
            slope = steep * upper_slope
            records.append((base, slope, upper_base, upper_slope))
        follow = nothing
        joined[0, 0] = nothing
        joined[rad - 1, 1] = nothing
        for k in reversed(range(crossings)):
            base, slope, upper_base, upper_slope = records[k]
            joined[k + 1, 0] = rates[k] * (base + slope * follow)
            follow = upper_base + upper_slope * follow
            joined[k, 1] = rates[k] * follow
        before = joined[band, 0]
        beyond = joined[band, 1]
        for z in range(nth):
            block = g[z]
            out[nf - 1, z * rows : (z + 1) * rows, :] = (
                local[z] + block[:, :1] * before[z : z + 1] + block[:, rows - 1 :] * beyond[z : z + 1]
            )

    def prepare():
        for copy in params:
            copy.wait()

        def row(r, carry):
            speed[r] = raw_v[pl.ds(r, nth, stride=rows), :]
            return carry

        lax.fori_loop(0, rows, row, 0, unroll=8)
        speed_edge[...] = packed(lambda r: speed[r])
        speed_copy().start()
        sub = lax.broadcasted_iota(jnp.int32, (8, LANES), 0)
        table = jnp.zeros((8, LANES), F32)
        for z in range(nth):
            block = g[z]
            entries = [block[0:1, 0:1], block[0:1, rows - 1 :], block[rows - 1 :, 0:1], block[rows - 1 :, rows - 1 :]]
            for c, entry in enumerate(entries):
                table = jnp.where((sub == z) & (lane == c), entry, table)
            table = jnp.where((sub == z) & (lane == 4), link[z], table)
        corner[...] = table
        corner_in[band] = table
        to_bands(corner, corner_in, 0, True)

    for i in range(nf):
        stage(i)
    pl.semaphore_wait(barrier, az - 1 + rad - 1)
    for i in range(nf - 1):
        send_out(i)
    prepare()
    kept = []
    for i in range(nf):
        kept.append(rotate(i))
        if i == 0:
            send_home(i)
            send_out(nf - 1)
        elif i == 1:
            send_rims(0, kept[0] + kept[1])
            send_home(i)
        elif i < nf - 2:
            send_home(i)
        if i == nf - 2:
            send_home(i)
        if i == nf - 1:
            send_rims(1, sum(kept[2:], []))
            send_home(i)
        if i == 1:
            back_speed()
        if i == 3:
            opened = take_rims(0)
            advect(0, rims_of(opened, 0))
            solve_local()
        if i == 3:
            advect(1, rims_of(opened, 1))
    table = take_rims(1)
    for i in range(2, nf - 1):
        advect(i, rims_of(table, i - 2))
    interface()
    advect(nf - 1, rims_of(table, nf - 3))

    for i in range(nf):
        wait_bytes(staged.at[i, pl.ds(0, rows - own)], send_a.at[i])
        wait_bytes(turned.at[i, pl.ds(0, az - 1)], send_b.at[i])
    for n in range(nrims):
        wait_bytes(rim.at[n, pl.ds(0, az - 1)], send_e.at[n])
    wait_bytes(speed_edge, send_e.at[nrims])
    wait_bytes(corner_in.at[pl.ds(0, rad - 1)], send_r.at[0])
    wait_bytes(ends_in.at[pl.ds(0, rad - 1)], send_r.at[1])


def per_device(az, rad, fields, velocity, shifts, block_inverse, coupling):
    nf, nth, rows, lanes = fields.shape
    own = rows // az
    whole = nth * rows
    hbm = pl.BlockSpec(memory_space=pltpu.MemorySpace.HBM)
    vmem = pl.BlockSpec(memory_space=pltpu.MemorySpace.VMEM)
    dma = pltpu.SemaphoreType.DMA
    out = pl.pallas_call(
        functools.partial(kernel, az, rad, nf, rows),
        out_shape=jax.ShapeDtypeStruct((nf, whole, lanes), F32),
        in_specs=[hbm] * 5,
        out_specs=vmem,
        scratch_shapes=[
            pltpu.VMEM((nf, whole, lanes), F32),
            pltpu.VMEM((whole, lanes), F32),
            pltpu.VMEM((nth, rows, rows), F32),
            pltpu.VMEM((nf, rows, nth, lanes), F32),
            pltpu.VMEM((nf, az, own, nth, lanes), F32),
            pltpu.VMEM((nf, rows, nth, lanes), F32),
            pltpu.VMEM((rows, nth, lanes), F32),
            pltpu.VMEM((whole, lanes), F32),
            pltpu.VMEM((nth, rows, lanes), F32),
            pltpu.VMEM((2, az, 1, lanes), F32),
            pltpu.VMEM((2, az, 1, lanes), F32),
            pltpu.VMEM((nth, lanes), F32),
            pltpu.VMEM((nth, lanes), F32),
            pltpu.VMEM((rows, nth, lanes), F32),
            pltpu.VMEM((nth, lanes), F32),
            pltpu.VMEM((rad, nth, lanes), F32),
            pltpu.VMEM((2, nth, lanes), F32),
            pltpu.VMEM((rad, 2, nth, lanes), F32),
            pltpu.VMEM((rad, 2, nth, lanes), F32),
            pltpu.SMEM((rows,), jnp.int32),
            pltpu.SMEM((nth,), F32),
            dma((nf,)),
            dma((4,)),
            dma((nf,)),
            dma((nf,)),
            dma((nf,)),
            dma((nf,)),
            dma((3,)),
            dma((3,)),
            dma((2,)),
            dma((2,)),
        ]
        + [pltpu.VMEM((az, own, nth, lanes), F32)] * nf,
        compiler_params=pltpu.CompilerParams(
            collective_id=0, has_side_effects=True, vmem_limit_bytes=40 << 20
        ),
    )(
        *(
            pltpu.with_memory_space_constraint(x, pltpu.MemorySpace.HBM)
            for x in (
                fields.reshape(nf, whole, lanes),
                velocity.reshape(whole, lanes),
                shifts,
                block_inverse,
                coupling.reshape(nth),
            )
        )
    )
    return out.reshape(fields.shape)


def solution(mesh):
    placed = (
        P(None, None, "rad", "az"),
        P(None, "rad", "az"),
        P("rad"),
        P(None, "rad", None),
        P(None, "rad"),
    )
    return jax.shard_map(
        functools.partial(per_device, mesh.shape["az"], mesh.shape["rad"]),
        mesh=mesh,
        in_specs=placed,
        out_specs=P(None, None, "rad", "az"),
        check_vma=False,
    )
```

```python
import functools

import jax
import jax.numpy as jnp
from jax import lax
from jax.experimental import pallas as pl
from jax.experimental.pallas import tpu as pltpu
from jax.sharding import PartitionSpec as P

MESH = pl.DeviceIdType.MESH
LANES = 128
F32 = jnp.float32


def lane_index():
    return lax.broadcasted_iota(jnp.int32, (8, LANES), 1)


def kernel(az, rad, nf, rows, *refs):
    nth = 8
    own = rows // az
    order = [nf - 1] + list(range(nf - 1))
    nrims = 2
    half = az // 2
    (f_hbm, v_hbm, shifts_hbm, g_hbm, link_hbm, out) = refs[:6]
    (raw, raw_v, g, staged, turned, arrived, speed, energy, local) = refs[6:15]
    (rim, rim_in, speed_edge, speed_edge_in, speed_back) = refs[15:20]
    (corner, corner_in, ends, ends_in, joined) = refs[20:25]
    (shifts, link) = refs[25:27]
    (in_sem, par_sem, send_a, recv_a, send_b, recv_b, send_e, recv_e, send_r, recv_r) = refs[27:37]
    homes = refs[37 : 37 + nf]

    me = lax.axis_index("az")
    band = lax.axis_index("rad")
    right = lax.rem(me + 1, az)
    left = lax.rem(me + az - 1, az)
    lane = lane_index()

    loads = [pltpu.make_async_copy(f_hbm.at[f], raw.at[i], in_sem.at[i]) for i, f in enumerate(order)]
    params = [
        pltpu.make_async_copy(v_hbm, raw_v, par_sem.at[0]),
        pltpu.make_async_copy(g_hbm, g, par_sem.at[1]),
        pltpu.make_async_copy(shifts_hbm, shifts, par_sem.at[2]),
        pltpu.make_async_copy(link_hbm, link, par_sem.at[3]),
    ]
    loads[0].start()

    barrier = pltpu.get_barrier_semaphore()

    def greet_az(k, carry):
        pl.semaphore_signal(barrier, 1, device_id={"az": lax.rem(me + k, az), "rad": band}, device_id_type=MESH)
        return carry

    def greet_rad(k, carry):
        pl.semaphore_signal(barrier, 1, device_id={"az": me, "rad": lax.rem(band + k, rad)}, device_id_type=MESH)
        return carry

    lax.fori_loop(1, az, greet_az, 0)
    lax.fori_loop(1, rad, greet_rad, 0)
    for copy in loads[1:] + params:
        copy.start()

    def stage(i):
        loads[i].wait()

        def row(r, carry):
            staged[i, r] = raw[i, pl.ds(r, nth, stride=rows), :]
            return carry

        lax.fori_loop(0, rows, row, 0, unroll=8)

    def send_out(i):
        def to(k, carry):
            m = lax.rem(me + k, az)
            pltpu.make_async_remote_copy(
                staged.at[i, pl.ds(m * own, own)],
                homes[i].at[me],
                send_a.at[i],
                recv_a.at[i],
                device_id={"az": m, "rad": band},
                device_id_type=MESH,
            ).start()
            return carry

        lax.fori_loop(1, az, to, 0)
        homes[i][me] = staged[i, pl.ds(me * own, own)]

    def wait_bytes(ref, sem):
        pltpu.make_async_copy(ref, ref, sem).wait()

    def rotate(i):
        wait_bytes(homes[i].at[pl.ds(0, az - 1)], recv_a.at[i])
        shift = [shifts[me * own + j] for j in range(own)]
        hops = [lax.shift_right_logical(v, 7) for v in shift]
        rest = [jnp.bitwise_and(v, LANES - 1) for v in shift]
        carried = [lane >= v for v in rest]

        def turn(b, j):
            return pltpu.roll(homes[i][jnp.bitwise_and(b + az - hops[j], az - 1), j], rest[j], 1)

        def block(b, carry):
            ahead = jnp.bitwise_and(b + 1, az - 1)
            behind = jnp.bitwise_and(b + az - 1, az - 1)
            made = []
            for j in range(own):
                previous, lefts, rights = carry[j]
                current = turn(b, j)
                value = jnp.where(carried[j], current, previous)
                turned[i, b, j] = value
                lefts = jnp.where(lane == ahead, pltpu.roll(value, ahead + 1, 1), lefts)
                rights = jnp.where(lane == behind, pltpu.roll(value, behind, 1), rights)
                made.append((current, lefts, rights))
            return tuple(made)

        zero = jnp.zeros((8, LANES), F32)
        opening = tuple((turn(az - 1, j), zero, zero) for j in range(own))
        done = lax.fori_loop(0, az, block, opening, unroll=4)
        return [tile for j in range(own) for tile in done[j][1:]]

    def send_home(i):
        def to(k, carry, near=True):
            m = lax.rem(me + k, az)
            pltpu.make_async_remote_copy(
                turned.at[i, m],
                arrived.at[i, pl.ds(me * own, own)],
                send_b.at[i],
                recv_b.at[i if near else nf],
                device_id={"az": m, "rad": band},
                device_id_type=MESH,
            ).start()
            return carry

        if i == nf - 1:
            lax.fori_loop(1, half, to, 0)
            lax.fori_loop(half, az, functools.partial(to, near=False), 0)
        else:
            lax.fori_loop(1, az, to, 0)
        arrived[i, pl.ds(me * own, own)] = turned[i, me]

    key = jnp.bitwise_and(lax.shift_right_logical(lane + 1, 1), LANES // 2 - 1)

    def packed(load):
        def row(r, carry):
            return jnp.where(key == r, pltpu.roll(load(r), 2 * r, 1), carry)

        return lax.fori_loop(0, rows, row, jnp.zeros((8, LANES), F32), unroll=8)

    def send_rims(n, tiles):
        tiles = tiles + [jnp.zeros((8, LANES), F32)] * (LANES // 8 - len(tiles))
        rows_out = jnp.transpose(jnp.concatenate(tiles, axis=0))
        for b in range(az):
            rim[n, b] = rows_out[b : b + 1]

        def to(k, carry):
            m = lax.rem(me + k, az)
            pltpu.make_async_remote_copy(
                rim.at[n, m],
                rim_in.at[n, me],
                send_e.at[n],
                recv_e.at[n],
                device_id={"az": m, "rad": band},
                device_id_type=MESH,
            ).start()
            return carry

        lax.fori_loop(1, az, to, 0)
        rim_in[n, me] = rim[n, me]

    def take_rims(n):
        wait_bytes(rim_in.at[n, pl.ds(0, az - 1)], recv_e.at[n])
        tiles = [rim_in[n, m] for m in range(az)] + [jnp.zeros((LANES - az, LANES), F32)]
        return jnp.transpose(jnp.concatenate(tiles, axis=0))

    def speed_copy():
        return pltpu.make_async_remote_copy(
            speed_edge,
            speed_edge_in,
            send_e.at[nrims],
            recv_e.at[nrims],
            device_id={"az": right, "rad": band},
            device_id_type=MESH,
        )

    def to_bands(source, target, which, start):
        def to(k, carry):
            copy = pltpu.make_async_remote_copy(
                source,
                target.at[band],
                send_r.at[which],
                recv_r.at[which],
                device_id={"az": me, "rad": lax.rem(band + k, rad)},
                device_id_type=MESH,
            )
            copy.start()
            return carry

        lax.fori_loop(1, rad, to, 0)

    def advect(i, rims):
        def home(k, carry):
            m = lax.rem(me + az - k, az)
            for j in range(own):
                r = m * own + j
                value = arrived[i, r]
                rate, rate_back = speed[r], speed_back[r]
                left, right = rims[2 * j], rims[2 * j + 1]
                ahead = jnp.where(
                    lane == LANES - 1, pltpu.roll(right, LANES - 1 - m, 1), pltpu.roll(value, LANES - 1, 1)
                )
                back = jnp.where(
                    lane == 0, pltpu.roll(left, jnp.bitwise_and(LANES - m, LANES - 1), 1), pltpu.roll(value, 1, 1)
                )
                outflow = jnp.maximum(rate, 0.0) * value + jnp.minimum(rate, 0.0) * ahead
                inflow = jnp.maximum(rate_back, 0.0) * back + jnp.minimum(rate_back, 0.0) * value
                moved = value - (outflow - inflow)
                if i == 0:
                    energy[pl.ds(r, nth, stride=rows), :] = moved
                else:
                    out[order[i], pl.ds(r, nth, stride=rows), :] = moved
            return carry

        if i == nf - 1:
            wait_bytes(arrived.at[i, pl.ds(0, (half - 1) * own)], recv_b.at[i])
            lax.fori_loop(0, half, home, 0, unroll=8)
            wait_bytes(arrived.at[i, pl.ds(0, (az - half) * own)], recv_b.at[nf])
            lax.fori_loop(half, az, home, 0, unroll=8)
        else:
            wait_bytes(arrived.at[i, pl.ds(0, rows - own)], recv_b.at[i])
            lax.fori_loop(0, az, home, 0, unroll=8)

    def rims_of(table, place):
        at = place * 2 * own * 8
        return [table[at + 8 * c : at + 8 * (c + 1)] for c in range(2 * own)]

    def back_speed():
        wait_bytes(speed_edge_in, recv_e.at[nrims])

        def row(r, carry):
            entry = pltpu.roll(speed_edge_in[...], jnp.bitwise_and(LANES + 1 - 2 * r, LANES - 1), 1)
            speed_back[r] = jnp.where(lane == 0, entry, pltpu.roll(speed[r], 1, 1))
            return carry

        lax.fori_loop(0, rows, row, 0, unroll=8)

    def solve_local():
        for z in range(nth):
            part = jnp.dot(
                g[z],
                energy[z * rows : (z + 1) * rows, :],
                precision=lax.Precision.HIGHEST,
                preferred_element_type=F32,
            )
            local[z] = part
            ends[0, z : z + 1, :] = part[:1]
            ends[1, z : z + 1, :] = part[rows - 1 :]
        ends_in[band] = ends[...]
        to_bands(ends, ends_in, 1, True)

    def interface():
        wait_bytes(corner_in.at[pl.ds(0, rad - 1)], recv_r.at[0])
        wait_bytes(ends_in.at[pl.ds(0, rad - 1)], recv_r.at[1])
        top_left, top_right, low_left, low_right, rates = (
            [corner_in[k][:, c : c + 1] for k in range(rad)] for c in range(5)
        )
        crossings = rad - 1
        zero = jnp.zeros((8, 1), F32)
        nothing = jnp.zeros((8, LANES), F32)
        base, slope = nothing, zero
        records = []
        for k in range(crossings):
            back = rates[k - 1] * low_left[k] if k > 0 else zero
            here = rates[k] * low_right[k]
            fore = rates[k] * top_left[k + 1]
            onward = rates[k + 1] * top_right[k + 1] if k + 1 < crossings else zero
            steep = back * slope + here
            offset = ends_in[k, 1] + back * base
            scale = 1.0 - fore * steep
            upper_base = (ends_in[k + 1, 0] + fore * offset) / scale
            upper_slope = onward / scale
            base = offset + steep * upper_base
            slope = steep * upper_slope
            records.append((base, slope, upper_base, upper_slope))
        follow = nothing
        joined[0, 0] = nothing
        joined[rad - 1, 1] = nothing
        for k in reversed(range(crossings)):
            base, slope, upper_base, upper_slope = records[k]
            joined[k + 1, 0] = rates[k] * (base + slope * follow)
            follow = upper_base + upper_slope * follow
            joined[k, 1] = rates[k] * follow
        before = joined[band, 0]
        beyond = joined[band, 1]
        for z in range(nth):
            block = g[z]
            out[nf - 1, z * rows : (z + 1) * rows, :] = (
                local[z] + block[:, :1] * before[z : z + 1] + block[:, rows - 1 :] * beyond[z : z + 1]
            )

    def prepare():
        for copy in params:
            copy.wait()

        def row(r, carry):
            speed[r] = raw_v[pl.ds(r, nth, stride=rows), :]
            return carry

        lax.fori_loop(0, rows, row, 0, unroll=8)
        speed_edge[...] = packed(lambda r: speed[r])
        speed_copy().start()
        sub = lax.broadcasted_iota(jnp.int32, (8, LANES), 0)
        table = jnp.zeros((8, LANES), F32)
        for z in range(nth):
            block = g[z]
            entries = [block[0:1, 0:1], block[0:1, rows - 1 :], block[rows - 1 :, 0:1], block[rows - 1 :, rows - 1 :]]
            for c, entry in enumerate(entries):
                table = jnp.where((sub == z) & (lane == c), entry, table)
            table = jnp.where((sub == z) & (lane == 4), link[z], table)
        corner[...] = table
        corner_in[band] = table
        to_bands(corner, corner_in, 0, True)

    stage(0)
    pl.semaphore_wait(barrier, az - 1 + rad - 1)
    send_out(0)
    for i in range(1, nf - 1):
        stage(i)
        send_out(i)
    prepare()
    stage(nf - 1)
    kept = []
    for i in range(nf):
        kept.append(rotate(i))
        if i == 0:
            send_home(i)
            send_out(nf - 1)
        elif i == 1:
            send_rims(0, kept[0] + kept[1])
            send_home(i)
        elif i < nf - 2:
            send_home(i)
        if i == nf - 2:
            send_home(i)
        if i == nf - 1:
            send_rims(1, sum(kept[2:], []))
            send_home(i)
        if i == 1:
            back_speed()
        if i == 3:
            opened = take_rims(0)
            advect(0, rims_of(opened, 0))
            solve_local()
        if i == 3:
            advect(1, rims_of(opened, 1))
    table = take_rims(1)
    for i in range(2, nf - 1):
        advect(i, rims_of(table, i - 2))
    interface()
    advect(nf - 1, rims_of(table, nf - 3))

    for i in range(nf):
        wait_bytes(staged.at[i, pl.ds(0, rows - own)], send_a.at[i])
        wait_bytes(turned.at[i, pl.ds(0, az - 1)], send_b.at[i])
    for n in range(nrims):
        wait_bytes(rim.at[n, pl.ds(0, az - 1)], send_e.at[n])
    wait_bytes(speed_edge, send_e.at[nrims])
    wait_bytes(corner_in.at[pl.ds(0, rad - 1)], send_r.at[0])
    wait_bytes(ends_in.at[pl.ds(0, rad - 1)], send_r.at[1])


def per_device(az, rad, fields, velocity, shifts, block_inverse, coupling):
    nf, nth, rows, lanes = fields.shape
    own = rows // az
    whole = nth * rows
    hbm = pl.BlockSpec(memory_space=pltpu.MemorySpace.HBM)
    vmem = pl.BlockSpec(memory_space=pltpu.MemorySpace.VMEM)
    dma = pltpu.SemaphoreType.DMA
    out = pl.pallas_call(
        functools.partial(kernel, az, rad, nf, rows),
        out_shape=jax.ShapeDtypeStruct((nf, whole, lanes), F32),
        in_specs=[hbm] * 5,
        out_specs=vmem,
        scratch_shapes=[
            pltpu.VMEM((nf, whole, lanes), F32),
            pltpu.VMEM((whole, lanes), F32),
            pltpu.VMEM((nth, rows, rows), F32),
            pltpu.VMEM((nf, rows, nth, lanes), F32),
            pltpu.VMEM((nf, az, own, nth, lanes), F32),
            pltpu.VMEM((nf, rows, nth, lanes), F32),
            pltpu.VMEM((rows, nth, lanes), F32),
            pltpu.VMEM((whole, lanes), F32),
            pltpu.VMEM((nth, rows, lanes), F32),
            pltpu.VMEM((2, az, 1, lanes), F32),
            pltpu.VMEM((2, az, 1, lanes), F32),
            pltpu.VMEM((nth, lanes), F32),
            pltpu.VMEM((nth, lanes), F32),
            pltpu.VMEM((rows, nth, lanes), F32),
            pltpu.VMEM((nth, lanes), F32),
            pltpu.VMEM((rad, nth, lanes), F32),
            pltpu.VMEM((2, nth, lanes), F32),
            pltpu.VMEM((rad, 2, nth, lanes), F32),
            pltpu.VMEM((rad, 2, nth, lanes), F32),
            pltpu.SMEM((rows,), jnp.int32),
            pltpu.SMEM((nth,), F32),
            dma((nf,)),
            dma((4,)),
            dma((nf,)),
            dma((nf,)),
            dma((nf,)),
            dma((nf + 1,)),
            dma((3,)),
            dma((3,)),
            dma((2,)),
            dma((2,)),
        ]
        + [pltpu.VMEM((az, own, nth, lanes), F32)] * nf,
        compiler_params=pltpu.CompilerParams(
            collective_id=0, has_side_effects=True, vmem_limit_bytes=40 << 20
        ),
    )(
        *(
            pltpu.with_memory_space_constraint(x, pltpu.MemorySpace.HBM)
            for x in (
                fields.reshape(nf, whole, lanes),
                velocity.reshape(whole, lanes),
                shifts,
                block_inverse,
                coupling.reshape(nth),
            )
        )
    )
    return out.reshape(fields.shape)


def solution(mesh):
    placed = (
        P(None, None, "rad", "az"),
        P(None, "rad", "az"),
        P("rad"),
        P(None, "rad", None),
        P(None, "rad"),
    )
    return jax.shard_map(
        functools.partial(per_device, mesh.shape["az"], mesh.shape["rad"]),
        mesh=mesh,
        in_specs=placed,
        out_specs=P(None, None, "rad", "az"),
        check_vma=False,
    )
```
